32 devices in a mesh: groups: 2 (over y), seq: 4 (over z), chan: 4 (over x, core).
Axes of the slice: x: 2, y: 2, z: 4, core: 2. Of those that a mesh axis runs over, the one named last changes fastest.
Arguments:
- x_rows: bfloat16 [40, 96, 1536], P(('groups', 'seq'), None, 'chan'), parts along dimension 0, may hold values from -6 to 6
- dest_slab: int32 [40], P(('groups', 'seq')), parts along dimension 0, may hold values from 0 to 4, as said below
- kept_len: int32 [40], P(('groups', 'seq')), parts along dimension 0, may hold values from 1 to 96
- convolution_weight: bfloat16 [1536, 5, 1536], P(None, None, 'chan'), may hold values from -0.0625 to 0.0625
- b_conv: float32 [1536], P('chan'), may hold values from -3 to 3
- entry_norm_gain: float32 [1536], P('chan'), may hold values from 0.1 to 1.9
- w_proj: bfloat16 [1024, 1536], P(None, 'chan'), may hold values from -0.15625 to 0.15625
- g_cot: bfloat16 [1024, 1536], P(('seq', 'chan'), 'groups'), parts along dimension 1, may hold values from -6 to 6
Outputs:
- qk_out: bfloat16 [1024, 1536], P(('seq', 'chan'), 'groups'), parts along dimension 1
- dw_conv: float32 [3072, 5, 1536], P(('groups', 'seq'), None, 'chan'), parts along dimension 0
- dw_proj: float32 [2048, 1536], P(('groups', 'seq'), 'chan'), parts along dimension 0
- dx_field: bfloat16 [1536, 3072], P('chan', ('groups', 'seq')), parts along dimension 1
The draws below stay inside these ranges and needn't reach their ends.
There are 2 independent parts, one for each index of `groups`. The reference program is written for one: setup_inputs(seed, part) draws one part's arguments, and reference() takes and returns one part's arrays. A program takes and returns all parts, laid end to end along the dimension named above; an argument that names none is the same for every part. Nothing has to cross between parts.
Inputs may be any that keep to these rules, and one draw needn't show every extreme that they name: `dest_slab`: each slab 0 to 3 is named by exactly 4 blocks; the blocks of one device name each slab at most 2 times, and in every draw some device names some slab exactly 2 times; every device holds exactly 1 block marked 4.
All inputs are finite; a program needn't handle non-finite values.
Results may differ from the reference program's by a relative error of at most 0.005.
Values may be sent and summed in bfloat16 or wider, within the bound.
No kernel may reach another device: no remote copies, remote signals or barrier semaphores. Data moves between devices by JAX's collectives and lax.ppermute only.
A program may use at most 128 MiB of HBM per device.

```python
import jax
import jax.numpy as jnp
from jax import lax

C = 1536
KERNEL_TAPS = 5
DILATION_STEP = 2
SLAB = 384
F = 1024
ROWS_DEV = 4
BLK = 96
DROP_DEV = 1
SRC_DEV = 5
POS = 768
N_SEQ = 4


def draw_dest_slab(key, part):
    slab_count = N_SEQ
    key_src, key_dst, key_order = jax.random.split(jax.random.fold_in(key, 17), 3)
    src_perm = jax.random.permutation(key_src, slab_count).astype(jnp.int32)
    dst_perm = jax.random.permutation(key_dst, slab_count).astype(jnp.int32)
    ladder = jnp.arange(slab_count, dtype=jnp.int32)
    src_place = jnp.zeros((slab_count,), jnp.int32).at[src_perm].set(ladder)
    dst_place = jnp.zeros((slab_count,), jnp.int32).at[dst_perm].set(ladder)
    same_pair = src_place[:, None] // 2 == dst_place[None, :] // 2
    same_side = src_place[:, None] % 2 == dst_place[None, :] % 2
    pair_counts = jnp.where(same_pair, jnp.where(same_side, 2, 0), 1).astype(jnp.int32)
    ends = jnp.cumsum(pair_counts, axis=1)
    slot_ids = jnp.arange(ROWS_DEV, dtype=jnp.int32)
    dests = jnp.sum((ends[:, None, :] <= slot_ids[None, :, None]).astype(jnp.int32), axis=2)
    dropped = jnp.full((slab_count, DROP_DEV), slab_count, jnp.int32)
    rows_all = jnp.concatenate([dests, dropped], axis=1)
    row_keys = jax.random.split(key_order, slab_count)
    orders = jax.vmap(lambda one_key: jax.random.permutation(one_key, SRC_DEV))(row_keys)
    rows_all = jnp.take_along_axis(rows_all, orders.astype(jnp.int32), axis=1)
    return rows_all.reshape(-1).astype(jnp.int32)


def set_ends(entries, rng, smallest, top_value):
    extent = entries.shape
    place = [jax.random.randint(jax.random.fold_in(rng, axis), (), 0, extent[axis]) for axis in range(len(extent))]
    entries = entries.at[tuple(place)].set(smallest)
    longest = extent.index(max(extent))
    place[longest] = (place[longest] + 1) % extent[longest]
    return entries.at[tuple(place)].set(top_value)


def levels(rng, dims, shards, low, top_value):
    loudness, own = 1.0, jax.random.fold_in(rng, 6)
    for axis_at, parts in shards:
        steps = jnp.exp(jax.random.uniform(jax.random.fold_in(own, axis_at), (parts,), jnp.float32, low / len(shards), top_value / len(shards)))
        loudness = loudness * jnp.repeat(steps, dims[axis_at] // parts).reshape([-1 if axis == axis_at else 1 for axis in range(len(dims))])
    return loudness


def gaussian(own_key, extent, deviation, reach, cuts=(), kind=jnp.bfloat16):
    array = deviation * jax.random.normal(own_key, extent, jnp.float32)
    if cuts:
        array = array * levels(own_key, extent, cuts, -0.22, 0.18)
    return jnp.clip(array, -reach, reach).astype(kind)


def setup_inputs(seed: int = 0, part: int = 0) -> dict:
    splits = jax.random.split(jax.random.key(seed), 9)
    part_splits = jax.random.split(jax.random.fold_in(splits[8], part), 9)
    return {
        "x_rows": gaussian(part_splits[0], (N_SEQ * SRC_DEV, BLK, C), 1.0, 6.0, ((0, 4), (2, 4))),
        "dest_slab": draw_dest_slab(jax.random.fold_in(jax.random.fold_in(splits[8], part), 71), part),
        "kept_len": set_ends(jax.random.randint(part_splits[2], (N_SEQ * SRC_DEV,), 1, BLK + 1), jax.random.fold_in(part_splits[2], 1), 1, BLK).astype(jnp.int32),
        "convolution_weight": gaussian(splits[3], (C, KERNEL_TAPS, C), (C * KERNEL_TAPS) ** -0.5, 0.0625, ((2, 4),)),
        "b_conv": gaussian(splits[4], (C,), 0.5, 3.0, ((0, 4),), jnp.float32),
        "entry_norm_gain": jnp.clip(1.0 + 0.18 * jax.random.normal(splits[5], (C,), jnp.float32), 0.1, 1.9),
        "w_proj": gaussian(splits[6], (F, C), C ** -0.5, 0.15625, ((1, 4),)),
        "g_cot": gaussian(part_splits[7], (F, POS), 1.0, 6.0, ((0, 16),)),
    }


def smooth_gate(values):
    return jax.nn.gelu(values, approximate=True)

def reference(x_rows, dest_slab, kept_len, convolution_weight, b_conv, entry_norm_gain, w_proj, g_cot):
    total_rows, block_len, channels = x_rows.shape
    sequence_length = SLAB * N_SEQ
    window_width = 2 * DILATION_STEP
    positions = lax.broadcasted_iota(jnp.int32, (total_rows, block_len), 1)
    keep_mask = (positions < kept_len[:, None]).astype(x_rows.dtype)
    masked = x_rows * keep_mask[:, :, None]
    slab_ids = jnp.arange(N_SEQ, dtype=jnp.int32)
    onehot = (dest_slab[:, None] == slab_ids[None, :]).astype(jnp.int32)
    before = jnp.cumsum(onehot, axis=0) - onehot
    rank_row = lax.optimization_barrier(jnp.sum(before * onehot, axis=1)).astype(jnp.int32)
    target = (dest_slab * ROWS_DEV + rank_row).astype(jnp.int32)
    routed = jnp.zeros((N_SEQ * ROWS_DEV, block_len, channels), x_rows.dtype)
    routed = routed.at[target].set(masked, mode='drop').reshape(sequence_length, channels)
    padded_input = jnp.pad(routed, ((window_width, window_width), (0, 0)))
    convolved = jnp.zeros((sequence_length, channels), jnp.float32)
    for kernel_tap_index in range(KERNEL_TAPS):
        convolved = convolved + jnp.dot(padded_input[kernel_tap_index * DILATION_STEP:kernel_tap_index * DILATION_STEP + sequence_length], convolution_weight[:, kernel_tap_index, :], preferred_element_type=jnp.float32)
    shifted = convolved + b_conv[None, :]
    act, gate_pull = jax.vjp(smooth_gate, shifted)
    paired = act.reshape(sequence_length // 2, 2, channels)
    pooled_output = (paired[:, 0, :] + paired[:, 1, :]) * 0.5
    mean_value = lax.optimization_barrier(jnp.mean(pooled_output, axis=1))
    mean_sq = lax.optimization_barrier(jnp.mean(pooled_output * pooled_output, axis=1))
    inverse_deviation = lax.rsqrt(mean_sq - mean_value * mean_value + 1e-05)
    centered_input = (pooled_output - mean_value[:, None]) * inverse_deviation[:, None]
    normalized = (centered_input * entry_norm_gain[None, :]).astype(jnp.bfloat16)
    qk_out = jnp.dot(w_proj, normalized.T, preferred_element_type=jnp.float32).astype(jnp.bfloat16)
    dnormed = jnp.dot(g_cot.T, w_proj, preferred_element_type=jnp.float32)
    dw_proj = jnp.dot(g_cot, normalized, preferred_element_type=jnp.float32)
    normalized_gradient = dnormed * entry_norm_gain[None, :]
    leading_mean = lax.optimization_barrier(jnp.mean(normalized_gradient, axis=1))
    trailing_mean = lax.optimization_barrier(jnp.mean(normalized_gradient * centered_input, axis=1))
    pooled_gradient = inverse_deviation[:, None] * (normalized_gradient - leading_mean[:, None] - centered_input * trailing_mean[:, None])
    dact = jnp.repeat(pooled_gradient * 0.5, 2, axis=0)
    output_gradient = gate_pull(dact)[0].astype(jnp.bfloat16)
    kernel_gradient = []
    for kernel_tap_index in range(KERNEL_TAPS):
        kernel_gradient.append(jnp.dot(padded_input[kernel_tap_index * DILATION_STEP:kernel_tap_index * DILATION_STEP + sequence_length].T, output_gradient, preferred_element_type=jnp.float32))
    dw_conv = jnp.stack(kernel_gradient, axis=1)
    dy_pad = jnp.pad(output_gradient, ((window_width, window_width), (0, 0)))
    input_grad = jnp.zeros((channels, sequence_length), jnp.float32)
    for kernel_tap_index in range(KERNEL_TAPS):
        shift_amount = (KERNEL_TAPS - 1 - kernel_tap_index) * DILATION_STEP
        input_grad = input_grad + jnp.dot(convolution_weight[:, kernel_tap_index, :], dy_pad[shift_amount:shift_amount + sequence_length].T, preferred_element_type=jnp.float32)
    dx_field = input_grad.astype(jnp.bfloat16)
    return (qk_out, dw_conv, dw_proj, dx_field)
```

```python
import jax
import jax.numpy as jnp
from jax import lax
from jax.sharding import PartitionSpec as P

KERNEL_TAPS = 5
DILATION_STEP = 2
CAP = 2


def padded(cells, sides, width):
    for axis, dim in sides:
        count = lax.axis_size(axis)
        ends = count - 1
        head = lax.slice_in_dim(cells, 0, width, axis=dim)
        tail = lax.slice_in_dim(cells, cells.shape[dim] - width, cells.shape[dim], axis=dim)
        cells = jnp.concatenate(
            [
                lax.ppermute(tail, axis, [(i, (i + 1) % count) for i in range(ends)]),
                cells,
                lax.ppermute(head, axis, [((i + 1) % count, i) for i in range(ends)]),
            ],
            axis=dim,
        )
    return cells


def smooth_gate(values):
    return jax.nn.gelu(values, approximate=True)


def per_device(
    x_rows, dest_slab, kept_len, convolution_weight, b_conv, entry_norm_gain, w_proj, g_cot
):
    seq_count = lax.axis_size("seq")
    chan_count = lax.axis_size("chan")
    src_rows, block_len, shard_ch = x_rows.shape
    every_channel = shard_ch * chan_count
    window_width = 2 * DILATION_STEP
    positions = lax.broadcasted_iota(jnp.int32, (src_rows, block_len), 1)
    keep_mask = (positions < kept_len[:, None]).astype(x_rows.dtype)
    masked = (x_rows * keep_mask[:, :, None]).reshape(src_rows, block_len * shard_ch)
    slab_ids = jnp.arange(seq_count + 1, dtype=jnp.int32)
    onehot = (dest_slab[:, None] == slab_ids[None, :]).astype(jnp.int32)
    row_ids = jnp.arange(src_rows, dtype=jnp.int32)
    same = (dest_slab[:, None] == dest_slab[None, :]) & (row_ids[None, :] < row_ids[:, None])
    slot_row = jnp.sum(same.astype(jnp.int32), axis=1)
    target = dest_slab * CAP + slot_row
    send_ids = jnp.arange(seq_count * CAP, dtype=jnp.int32)
    picker = (send_ids[:, None] == target[None, :]).astype(jnp.bfloat16)
    outgoing = jnp.dot(picker, masked, preferred_element_type=jnp.float32).astype(jnp.bfloat16)
    outgoing = outgoing.reshape(seq_count, CAP, block_len * shard_ch)
    sent_counts = jnp.sum(onehot[:, :seq_count], axis=0).astype(jnp.bfloat16).reshape(seq_count, 1)
    arrived, arrived_counts = (
        lax.all_to_all(outgoing, "seq", split_axis=0, concat_axis=0, tiled=True),
        lax.all_to_all(sent_counts, "seq", split_axis=0, concat_axis=0, tiled=True),
    )
    got_counts = arrived_counts[:, 0].astype(jnp.int32)
    src_ids = jnp.arange(seq_count, dtype=jnp.int32)
    offsets = jnp.sum(jnp.where(src_ids[None, :] < src_ids[:, None], got_counts[None, :], 0), axis=1)
    slot_ladder = jnp.arange(CAP, dtype=jnp.int32)
    placed = offsets[:, None] + slot_ladder[None, :]
    placed = jnp.where(slot_ladder[None, :] < got_counts[:, None], placed, -1).reshape(-1)
    block_ids = jnp.arange(seq_count, dtype=jnp.int32)
    arranger = (block_ids[:, None] == placed[None, :]).astype(jnp.bfloat16)
    routed = jnp.dot(
        arranger,
        arrived.reshape(seq_count * CAP, block_len * shard_ch),
        preferred_element_type=jnp.float32,
    )
    routed = routed.astype(jnp.bfloat16).reshape(seq_count * block_len, shard_ch)
    window_length = routed.shape[0]
    pooled_len = window_length // 2
    padded_input = padded(routed, (("seq", 0),), window_width)
    complete_rows = lax.all_gather(padded_input, "chan", axis=1, tiled=True)
    convolved = jnp.zeros((window_length, shard_ch), jnp.float32)
    for kernel_tap_index in range(KERNEL_TAPS):
        convolved = convolved + jnp.dot(
            complete_rows[
                kernel_tap_index * DILATION_STEP : kernel_tap_index * DILATION_STEP + window_length
            ],
            convolution_weight[:, kernel_tap_index, :],
            preferred_element_type=jnp.float32,
        )
    shifted = convolved + b_conv[None, :]
    act, gate_pull = jax.vjp(smooth_gate, shifted)
    paired = act.reshape(pooled_len, 2, shard_ch)
    pooled_output = (paired[:, 0, :] + paired[:, 1, :]) * 0.5
    feat_total = w_proj.shape[0]
    group_feat = feat_total // (seq_count * chan_count)
    block_feat = group_feat * chan_count
    cot_parts = lax.all_to_all(
        g_cot.reshape(group_feat, seq_count, pooled_len), "seq", split_axis=1, concat_axis=0, tiled=True
    ).reshape(seq_count, group_feat, pooled_len)
    cot_slab = lax.all_gather(cot_parts, "chan", axis=1, tiled=True).reshape(feat_total, pooled_len)
    cot_wide = lax.all_gather(g_cot, "chan", axis=0, tiled=True)
    dnormed = jnp.einsum("fp,fd->pd", cot_slab, w_proj, preferred_element_type=jnp.float32)
    dxhat = dnormed * entry_norm_gain[None, :]
    sums = lax.psum(
        jnp.stack(
            [
                jnp.sum(pooled_output, axis=1),
                jnp.sum(pooled_output * pooled_output, axis=1),
                jnp.sum(dxhat, axis=1),
                jnp.sum(dxhat * pooled_output, axis=1),
            ]
        ),
        "chan",
    ) / every_channel
    mean_value = sums[0]
    inverse_deviation = lax.rsqrt(sums[1] - mean_value * mean_value + 1e-05)
    leading = sums[2]
    trailing = inverse_deviation * (sums[3] - mean_value * leading)
    centered_input = (pooled_output - mean_value[:, None]) * inverse_deviation[:, None]
    normalized = (centered_input * entry_norm_gain[None, :]).astype(jnp.bfloat16)
    pooled_gradient = inverse_deviation[:, None] * (
        dxhat - leading[:, None] - centered_input * trailing[:, None]
    )
    dact = jnp.repeat(pooled_gradient * 0.5, 2, axis=0)
    output_gradient = gate_pull(dact)[0].astype(jnp.bfloat16)
    norm_all = lax.all_gather(normalized, "seq", axis=0, tiled=True)
    dy_all = lax.all_gather(output_gradient, "seq", axis=0, tiled=True)
    own_ch = every_channel // seq_count
    x_own = lax.all_to_all(
        complete_rows.reshape(-1, seq_count, own_ch), "seq", split_axis=1, concat_axis=0, tiled=True
    ).reshape(seq_count, -1, own_ch)
    dw_proj = jnp.dot(cot_wide, norm_all, preferred_element_type=jnp.float32)
    w_block = lax.dynamic_slice_in_dim(w_proj, lax.axis_index("seq") * block_feat, block_feat, axis=0)
    qk_part = jnp.einsum("fd,pd->fp", w_block, norm_all, preferred_element_type=jnp.float32)
    qk_out = lax.psum_scatter(qk_part, "chan", scatter_dimension=0, tiled=True).astype(jnp.bfloat16)
    dy_pad = padded(output_gradient, (("seq", 0),), window_width)
    total = jnp.zeros((shard_ch * lax.axis_size("chan"), window_length), jnp.float32)
    for kernel_tap_index in range(KERNEL_TAPS):
        shift_amount = (KERNEL_TAPS - 1 - kernel_tap_index) * DILATION_STEP
        total = total + jnp.einsum(
            "io,po->ip",
            convolution_weight[:, kernel_tap_index, :],
            dy_pad[shift_amount : shift_amount + window_length],
            preferred_element_type=jnp.float32,
        )
    pieces = lax.all_to_all(
        total.astype(jnp.bfloat16).reshape(chan_count, shard_ch, window_length), "chan", split_axis=0, concat_axis=0, tiled=True
    )
    dx_field = jnp.sum(pieces.astype(jnp.float32), axis=0).astype(jnp.bfloat16)
    taps_out = []
    for kernel_tap_index in range(KERNEL_TAPS):
        begin = kernel_tap_index * DILATION_STEP
        taps_out.append(
            jnp.einsum(
                "pi,po->io",
                x_own[:, begin : begin + window_length].reshape(-1, own_ch),
                dy_all,
                preferred_element_type=jnp.float32,
            )
        )
    dw_conv = jnp.stack(taps_out, axis=1)
    return (qk_out, dw_conv, dw_proj, dx_field)


def solution(mesh):
    return jax.shard_map(
        per_device,
        mesh=mesh,
        in_specs=(
            P(("groups", "seq"), None, "chan"),
            P(("groups", "seq")),
            P(("groups", "seq")),
            P(None, None, "chan"),
            P("chan"),
            P("chan"),
            P(None, "chan"),
            P(("seq", "chan"), "groups"),
        ),
        out_specs=(
            P(("seq", "chan"), "groups"),
            P(("groups", "seq"), None, "chan"),
            P(("groups", "seq"), "chan"),
            P("chan", ("groups", "seq")),
        ),
        check_vma=False,
    )
```

```python
import functools

import jax
import jax.numpy as jnp
from jax import lax
from jax.experimental import pallas as pl
from jax.experimental.pallas import tpu as pltpu
from jax.sharding import PartitionSpec as P

KERNEL_TAPS = 5
DILATION_STEP = 2
CAP = 2
EDGE = 2 * DILATION_STEP
BF = jnp.bfloat16
F32 = jnp.float32
ROOT = 0.7978845608028654
CUBE = 0.044715

VMEM = pl.BlockSpec(memory_space=pltpu.VMEM)
SMEM = pl.BlockSpec(memory_space=pltpu.SMEM)
ANY = pl.BlockSpec(memory_space=pl.ANY)


def struct(shape, dtype):
    return jax.ShapeDtypeStruct(shape, dtype)


def launch(body, outs, ins, specs=None, scratch=(), flops=0, moved=0, name=None):
    return pl.pallas_call(
        body,
        out_shape=outs,
        in_specs=specs or [VMEM] * len(ins),
        out_specs=jax.tree.map(lambda _: VMEM, outs),
        scratch_shapes=list(scratch),
        compiler_params=pltpu.CompilerParams(vmem_limit_bytes=40 * 1024 * 1024),
        cost_estimate=pl.CostEstimate(flops=flops, bytes_accessed=moved, transcendentals=0),
        name=name,
    )(*ins)


def dot(a, b, dims=((1,), (0,))):
    return lax.dot_general(a, b, (dims, ((), ())), preferred_element_type=F32)


def wrap(value, count):
    return lax.rem(value + count, count)


def pack_kernel(slabs, rows, block_len, dest_ref, kept_ref, x_ref, *outs):
    me = lax.axis_index("seq")
    payload = outs[0].shape[0]
    dest = [jnp.where(dest_ref[r] >= slabs, -100, dest_ref[r]) for r in range(rows)]
    rank, total = [], []
    for r in range(rows):
        before, count = jnp.int32(0), jnp.int32(0)
        for q in range(rows):
            same = (dest[q] == dest[r]).astype(jnp.int32)
            count = count + same
            if q < r:
                before = before + same
        rank.append(before)
        total.append(count)
    columns = rows * block_len
    col = lax.broadcasted_iota(jnp.int32, (1, columns), 1)
    dest_v = jnp.full((1, columns), -100, jnp.int32)
    rank_v = jnp.zeros((1, columns), jnp.int32)
    last_v = jnp.zeros((1, columns), jnp.int32)
    place = jnp.zeros((1, columns), jnp.int32)
    for r in range(rows):
        offset = col - r * block_len
        here = (offset >= 0) & (offset < kept_ref[r]) & (offset < block_len)
        dest_v = jnp.where(here, dest[r], dest_v)
        rank_v = jnp.where(here, rank[r], rank_v)
        last_v = jnp.where(here, (rank[r] == total[r] - 1).astype(jnp.int32), last_v)
        place = jnp.where(here, offset, place)
    row = lax.broadcasted_iota(jnp.int32, (payload, columns), 0)
    line = lax.broadcasted_iota(jnp.int32, (payload, 1), 0)
    base = CAP * block_len
    x = x_ref[...]
    for k, out in enumerate(outs):
        to = wrap(me + k, slabs)
        key = jnp.where(dest_v == to, rank_v * block_len + place, -1)
        key = jnp.where((dest_v == to + 1) & (rank_v == 0) & (place < EDGE), base + place, key)
        tail = place - (block_len - EDGE)
        key = jnp.where((dest_v == to - 1) & (last_v == 1) & (tail >= 0), base + EDGE + tail, key)
        picker = jnp.where(row == key, 1.0, 0.0).astype(BF)
        rows_out = dot(picker, x)
        for spot, slab in enumerate((to, to - 1, to + 1)):
            count = jnp.int32(0)
            for r in range(rows):
                count = count + (dest[r] == slab).astype(jnp.int32)
            rows_out = jnp.where(line == base + 2 * EDGE + spot, count.astype(F32), rows_out)
        out[...] = rows_out.astype(BF)


def unpack_kernel(slabs, block_len, *refs):
    ins, out = refs[:slabs], refs[slabs]
    me = lax.axis_index("seq")
    payload = ins[0].shape[0]
    base = CAP * block_len
    length = slabs * block_len
    heads = [r[payload - 16 : payload, :].astype(F32) for r in ins]
    own = [h[2 * EDGE : 2 * EDGE + 1, :payload] for h in heads]
    prev = [h[2 * EDGE + 1 : 2 * EDGE + 2, :payload] for h in heads]
    following = [h[2 * EDGE + 2 : 2 * EDGE + 3, :payload] for h in heads]
    source = [wrap(me - k, slabs) for k in range(slabs)]
    col = lax.broadcasted_iota(jnp.int32, (1, payload), 1)
    slot = jnp.where(col >= block_len, 1, 0)
    place = (col - slot * block_len).astype(F32)
    slot = slot.astype(F32)
    colf = col.astype(F32)
    row = lax.broadcasted_iota(jnp.int32, out.shape[:1] + (payload,), 0).astype(F32)
    total = jnp.zeros(out.shape, F32)
    for k in range(slabs):
        offsets = []
        for counts in (own, prev, following):
            ahead = jnp.zeros((1, payload), F32)
            for q in range(slabs):
                if q != k:
                    ahead = ahead + jnp.where(source[q] < source[k], counts[q], 0.0)
            offsets.append(ahead)
        main = jnp.where(slot < own[k], (offsets[0] + slot) * block_len + place, -1.0)
        right = jnp.where((following[k] > 0.5) & (offsets[2] < 0.5), length + EDGE + colf - base, -1.0)
        left = jnp.where((prev[k] > 0.5) & (offsets[1] + prev[k] > slabs - 0.5), length + colf - base - EDGE, -1.0)
        key = jnp.where(col < base, main, jnp.where(col < base + EDGE, right, jnp.where(col < base + 2 * EDGE, left, -1.0)))
        total = total + dot(jnp.where(row == key, 1.0, 0.0).astype(BF), ins[k][...])
    out[...] = total.astype(BF)


def cot_kernel(slabs, chans, *refs):
    ins, (w_ref, gain_ref, out, full) = refs[:chans], refs[chans:]
    me, ch = lax.axis_index("seq"), lax.axis_index("chan")
    feat = ins[0].shape[1]
    for j in range(chans):
        owner = lax.bitwise_xor(ch, j)
        for k in range(slabs):
            begin = pl.multiple_of((wrap(me - k, slabs) * chans + owner) * feat, 8)
            full[pl.ds(begin, feat), :] = ins[j][k].astype(F32)
    out[...] = dot(full[...].astype(BF), w_ref[...], ((0,), (0,))) * gain_ref[...]


def conv_kernel(chans, slabs, *refs):
    xs, (w_ref, bias_ref, dxhat_ref, pooled_ref, slope_ref, stats_ref), rest = refs[:chans], refs[chans : chans + 6], refs[chans + 6 :]
    pieces, (weights, full, conv, shifted_sum, lanes, sems) = rest[:-6], rest[-6:]
    me, ch = lax.axis_index("seq"), lax.axis_index("chan")
    rows, width = xs[0].shape
    length = shifted_sum.shape[0]
    copies = []
    for t in range(KERNEL_TAPS):
        copies.append(pltpu.make_async_copy(w_ref.at[t], weights.at[t], sems.at[t]))
        copies[-1].start()
    for j in range(chans):
        begin = pl.multiple_of(lax.bitwise_xor(ch, j) * width, 128)
        full[:, pl.ds(begin, width)] = xs[j][...]
    part = length // chans
    begin = pl.multiple_of(ch * part, 8)
    own = width * chans // slabs
    if len(pieces) > 1:
        for k, piece in enumerate(pieces):
            first = pl.multiple_of(wrap(me + k, slabs) * own, 128)
            piece[...] = full[pl.ds(begin, part), pl.ds(first, own)]
    else:
        pieces[0][...] = full[pl.ds(begin, part), :]
    x = full[...]
    for t in range(KERNEL_TAPS):
        copies[t].wait()
        product = dot(x, weights[t])
        conv[0:EDGE] = product[length : length + EDGE]
        conv[EDGE : EDGE + length] = product[:length]
        conv[EDGE + length : 2 * EDGE + length] = product[length + EDGE : length + 2 * EDGE]
        moved = conv[t * DILATION_STEP : t * DILATION_STEP + length]
        if t == 0:
            shifted_sum[...] = moved + bias_ref[...]
        else:
            shifted_sum[...] += moved
    v = shifted_sum[...]
    th = jnp.tanh(ROOT * (v + CUBE * (v * v * v)))
    half = 0.5 * (1.0 + th)
    slope_ref[...] = half + (0.5 * ROOT) * v * (1.0 - th * th) * (1.0 + (3.0 * CUBE) * (v * v))
    act = v * half
    count = length // 2
    columns = []
    for c in range(width // 128):
        lanes[c] = act[:, c * 128 : (c + 1) * 128]
        columns.append((lanes[c, pl.ds(0, count, stride=2), :] + lanes[c, pl.ds(1, count, stride=2), :]) * 0.5)
    pooled = jnp.concatenate(columns, axis=1)
    pooled_ref[...] = pooled
    dxhat = dxhat_ref[...]
    sums = [
        jnp.sum(pooled, axis=1, keepdims=True),
        jnp.sum(pooled * pooled, axis=1, keepdims=True),
        jnp.sum(dxhat, axis=1, keepdims=True),
        jnp.sum(dxhat * pooled, axis=1, keepdims=True),
    ]
    lane = lax.broadcasted_iota(jnp.int32, (count, 128), 1)
    table = jnp.zeros((count, 128), F32)
    for n, s in enumerate(sums):
        table = jnp.where(lane == n, s, table)
    padded = stats_ref.shape[1]
    if padded > count:
        table = jnp.concatenate([table, jnp.zeros((padded - count, 128), F32)], axis=0)
    stats_ref[...] = table.T[:8]


def grad_kernel(chans, *refs):
    stats, (pooled_ref, slope_ref, dxhat_ref, gain_ref, normed_ref, dy_ref, head_ref, tail_ref, twice) = refs[:chans], refs[chans:]
    count, width = pooled_ref.shape
    total = stats[0][...]
    for s in stats[1:]:
        total = total + s[...]
    total = total * (1.0 / (width * chans))
    table = jnp.concatenate([total, jnp.zeros((120, total.shape[1]), F32)], axis=0).T[:count]
    mean = table[:, 0:1]
    rstd = lax.rsqrt(table[:, 1:2] - mean * mean + 1e-05)
    leading = table[:, 2:3]
    trailing = rstd * (table[:, 3:4] - mean * leading)
    xhat = (pooled_ref[...] - mean) * rstd
    normed_ref[...] = (xhat * gain_ref[...]).astype(BF)
    half = (0.5 * rstd) * (dxhat_ref[...] - leading - xhat * trailing)
    columns = []
    for c in range(width // 128):
        twice[c, pl.ds(0, count, stride=2), :] = half[:, c * 128 : (c + 1) * 128]
        twice[c, pl.ds(1, count, stride=2), :] = half[:, c * 128 : (c + 1) * 128]
        columns.append(twice[c])
    dy = (jnp.concatenate(columns, axis=1) * slope_ref[...]).astype(BF)
    dy_ref[...] = dy
    head_ref[...] = dy[:16]
    tail_ref[...] = dy[dy.shape[0] - 16 :]


def dx_kernel(chans, *refs):
    (dy_ref, left_ref, right_ref, w_ref), outs, (weights, wide, moved, sems) = refs[:4], refs[4 : 4 + chans], refs[4 + chans :]
    ch = lax.axis_index("chan")
    length, width = dy_ref.shape
    order = list(range(chans - 1, -1, -1))
    copies = []
    for j in order:
        begin = pl.multiple_of(lax.bitwise_xor(ch, j) * width, 16)
        copies.append(pltpu.make_async_copy(w_ref.at[:, pl.ds(begin, width), :], weights.at[j], sems.at[j]))
        copies[-1].start()
    wide[0:EDGE] = left_ref[...].astype(F32)[16 - EDGE :]
    wide[EDGE : EDGE + length] = dy_ref[...].astype(F32)
    wide[EDGE + length : 2 * EDGE + length] = right_ref[...].astype(F32)[:EDGE]
    for t in range(KERNEL_TAPS):
        begin = 2 * EDGE - t * DILATION_STEP
        moved[t] = wide[begin : begin + length].astype(BF)
    for n, j in enumerate(order):
        copies[n].wait()
        total = dot(weights[j, 0], moved[0], ((1,), (1,)))
        for t in range(1, KERNEL_TAPS):
            total = total + dot(weights[j, t], moved[t], ((1,), (1,)))
        outs[j][...] = total.astype(outs[j].dtype)


def transpose_kernel(slabs, chans, x_ref, out, full):
    me = lax.axis_index("seq")
    part = x_ref.shape[2]
    for j in range(chans):
        for k in range(slabs):
            begin = pl.multiple_of((wrap(me - k, slabs) * chans + j) * part, 8)
            full[pl.ds(begin, part), :] = x_ref[j, k]
    out[...] = full[...].T


def dw_kernel(slabs, *refs):
    xt_ref, dys, (out, full, moved) = refs[0], refs[1 : 1 + slabs], refs[1 + slabs :]
    me = lax.axis_index("seq")
    length, width = dys[0].shape
    every = length * slabs
    full[0:8] = jnp.zeros((8, width), F32)
    full[8 + every : 16 + every] = jnp.zeros((8, width), F32)
    for k in range(slabs):
        begin = pl.multiple_of(wrap(me - k, slabs) * length + 8, 8)
        full[pl.ds(begin, length), :] = dys[k][...].astype(F32)
    xt = xt_ref[...]
    for t in range(KERNEL_TAPS):
        begin = 8 + EDGE - t * DILATION_STEP
        moved[...] = full[begin : begin + every].astype(BF)
        out[t] = dot(xt, moved[...])


def proj_kernel(slabs, chans, *refs):
    cots, normed, (w_ref, dw_ref), outs, (wide, full, part) = (
        refs[:chans],
        refs[chans : chans + slabs],
        refs[chans + slabs : chans + slabs + 2],
        refs[chans + slabs + 2 : 2 * chans + slabs + 2],
        refs[2 * chans + slabs + 2 :],
    )
    me, ch = lax.axis_index("seq"), lax.axis_index("chan")
    feat = cots[0].shape[0]
    count = normed[0].shape[0]
    for j in range(chans):
        wide[pl.ds(pl.multiple_of(lax.bitwise_xor(ch, j) * feat, 8), feat), :] = cots[j][...]
    for k in range(slabs):
        full[pl.ds(pl.multiple_of(wrap(me - k, slabs) * count, 8), count), :] = normed[k][...]
    every = full[...]
    dw_ref[...] = dot(wide[...], every)
    rows = feat * chans
    part[...] = dot(w_ref[pl.ds(pl.multiple_of(me * rows, 8), rows), :], every, ((1,), (1,)))
    for j in range(chans):
        outs[j][...] = part[pl.ds(pl.multiple_of(lax.bitwise_xor(ch, j) * feat, 8), feat), :].astype(outs[j].dtype)


def swaps(value, count):
    return [value] + [lax.ppermute(value, "chan", [(i, i ^ j) for i in range(count)]) for j in range(1, count)]


def turn(value, k, count):
    return lax.ppermute(value, "seq", [(i, (i + k) % count) for i in range(count)]) if k else value


def gather_seq(value, count):
    if count <= 8:
        return [turn(value, k, count) for k in range(count)]
    every = lax.all_gather(value, "seq", axis=0, tiled=False)
    every = jnp.roll(every[::-1], lax.axis_index("seq") + 1, axis=0)
    return [every[k] for k in range(count)]


def trade_seq(values, count):
    if count <= 8:
        return [turn(v, k, count) for k, v in enumerate(values)]
    me = lax.axis_index("seq")
    sent = jnp.roll(jnp.stack(values), me, axis=0)
    got = lax.all_to_all(sent, "seq", split_axis=0, concat_axis=0, tiled=True)
    got = jnp.roll(got[::-1], me + 1, axis=0)
    return [got[k] for k in range(count)]


def per_device(x_rows, dest_slab, kept_len, convolution_weight, b_conv, entry_norm_gain, w_proj, g_cot):
    slabs = lax.axis_size("seq")
    chans = lax.axis_size("chan")
    rows, block_len, width = x_rows.shape
    channels = width * chans
    length = slabs * block_len
    count = length // 2
    payload = CAP * block_len + 16
    feat, positions = g_cot.shape
    padded_rows = length + 16
    taps = jnp.transpose(convolution_weight, (1, 0, 2))
    gain = entry_norm_gain.reshape(1, width)
    own = channels // slabs
    part = length // chans

    packed = launch(
        functools.partial(pack_kernel, slabs, rows, block_len),
        [struct((payload, width), BF)] * slabs,
        [dest_slab, kept_len, x_rows.reshape(rows * block_len, width)],
        specs=[SMEM, SMEM, VMEM],
        flops=2 * payload * slabs * rows * block_len * width,
        moved=2 * payload * slabs * width,
        name="pack",
    )
    arrived = trade_seq(packed, slabs)

    me = lax.axis_index("seq")
    cot_parts = [
        lax.dynamic_slice_in_dim(g_cot, wrap(me + k, slabs) * count, count, axis=1) for k in range(slabs)
    ]
    cot_mine = jnp.stack(trade_seq(cot_parts, slabs))
    cot_all = swaps(cot_mine, chans)
    cot_wide = swaps(g_cot, chans)
    dxhat = launch(
        functools.partial(cot_kernel, slabs, chans),
        struct((count, width), F32),
        [*cot_all, w_proj, gain],
        scratch=[pltpu.VMEM((feat * chans * slabs, count), F32)],
        flops=2 * feat * chans * slabs * count * width,
        moved=2 * feat * chans * slabs * (count + width),
        name="cotangent",
    )

    routed = launch(
        functools.partial(unpack_kernel, slabs, block_len),
        struct((padded_rows, width), BF),
        arrived,
        flops=2 * payload * slabs * padded_rows * width,
        moved=2 * payload * slabs * width,
        name="unpack",
    )
    x_all = swaps(routed, chans)
    small = slabs == chans
    piece_shapes = [struct((part, own), BF)] * slabs if small else [struct((part, channels), BF)]
    conv_outs = launch(
        functools.partial(conv_kernel, chans, slabs),
        [struct((count, width), F32), struct((length, width), F32), struct((8, -(-count // 128) * 128), F32), *piece_shapes],
        [*x_all, taps, b_conv.reshape(1, width), dxhat],
        specs=[VMEM] * chans + [ANY, VMEM, VMEM],
        scratch=[
            pltpu.VMEM((KERNEL_TAPS, channels, width), BF),
            pltpu.VMEM((padded_rows, channels), BF),
            pltpu.VMEM((length + 2 * EDGE, width), F32),
            pltpu.VMEM((length, width), F32),
            pltpu.VMEM((width // 128, length, 128), F32),
            pltpu.SemaphoreType.DMA((KERNEL_TAPS,)),
        ],
        flops=2 * padded_rows * channels * width * KERNEL_TAPS,
        moved=2 * channels * width * KERNEL_TAPS,
        name="conv",
    )
    pooled, slope, stats, pieces = conv_outs[0], conv_outs[1], conv_outs[2], conv_outs[3:]
    if small:
        mine = jnp.stack(trade_seq(pieces, slabs))
    else:
        mine = lax.all_to_all(pieces[0].reshape(part, slabs, own), "seq", split_axis=1, concat_axis=0, tiled=True)
        mine = jnp.roll(mine.reshape(slabs, part, own)[::-1], me + 1, axis=0)
    x_own = lax.all_gather(mine, "chan", axis=0, tiled=False)
    x_turned = launch(
        functools.partial(transpose_kernel, slabs, chans),
        struct((own, length * slabs), BF),
        [x_own],
        scratch=[pltpu.VMEM((length * slabs, own), BF)],
        moved=4 * own * length * slabs,
        name="turn_x",
    )

    normed, dy, head, tail = launch(
        functools.partial(grad_kernel, chans),
        [struct((count, width), BF), struct((length, width), BF), struct((16, width), BF), struct((16, width), BF)],
        [*swaps(stats, chans), pooled, slope, dxhat, gain],
        scratch=[pltpu.VMEM((width // 128, length, 128), F32)],
        flops=20 * length * width,
        moved=12 * length * width,
        name="gradient",
    )
    ends = slabs - 1
    from_left = lax.ppermute(tail, "seq", [(i, i + 1) for i in range(ends)])
    from_right = lax.ppermute(head, "seq", [(i + 1, i) for i in range(ends)])
    normed_all = gather_seq(normed, slabs)
    dy_all = gather_seq(dy, slabs)

    dx_parts = launch(
        functools.partial(dx_kernel, chans),
        [struct((width, length), F32)] + [struct((width, length), BF)] * (chans - 1),
        [dy, from_left, from_right, taps],
        specs=[VMEM, VMEM, VMEM, ANY],
        scratch=[
            pltpu.VMEM((chans, KERNEL_TAPS, width, width), BF),
            pltpu.VMEM((length + 2 * EDGE, width), F32),
            pltpu.VMEM((KERNEL_TAPS, length, width), BF),
            pltpu.SemaphoreType.DMA((chans,)),
        ],
        flops=2 * length * channels * width * KERNEL_TAPS,
        moved=2 * channels * width * KERNEL_TAPS,
        name="dx",
    )
    dx_sum = dx_parts[0]
    for j in range(1, chans):
        dx_sum = dx_sum + lax.ppermute(dx_parts[j], "chan", [(i, i ^ j) for i in range(chans)]).astype(F32)
    dx_field = dx_sum.astype(BF)

    proj = launch(
        functools.partial(proj_kernel, slabs, chans),
        [struct((feat * chans, width), F32), struct((feat, positions), F32)] + [struct((feat, positions), BF)] * (chans - 1),
        [*cot_wide, *normed_all, w_proj],
        scratch=[
            pltpu.VMEM((feat * chans, positions), BF),
            pltpu.VMEM((positions, width), BF),
            pltpu.VMEM((feat * chans, positions), F32),
        ],
        flops=4 * feat * chans * positions * width,
        moved=4 * feat * chans * width,
        name="projection",
    )
    dw_proj, qk_parts = proj[0], proj[1:]
    qk_sum = qk_parts[0]
    for j in range(1, chans):
        qk_sum = qk_sum + lax.ppermute(qk_parts[j], "chan", [(i, i ^ j) for i in range(chans)]).astype(F32)
    qk_out = qk_sum.astype(BF)

    dw_taps = launch(
        functools.partial(dw_kernel, slabs),
        struct((KERNEL_TAPS, own, width), F32),
        [x_turned, *dy_all],
        scratch=[pltpu.VMEM((length * slabs + 16, width), F32), pltpu.VMEM((length * slabs, width), BF)],
        flops=2 * length * slabs * own * width * KERNEL_TAPS,
        moved=4 * own * width * KERNEL_TAPS,
        name="dw",
    )
    return (qk_out, jnp.transpose(dw_taps, (1, 0, 2)), dw_proj, dx_field)


def solution(mesh):
    return jax.shard_map(
        per_device,
        mesh=mesh,
        in_specs=(
            P(("groups", "seq"), None, "chan"),
            P(("groups", "seq")),
            P(("groups", "seq")),
            P(None, None, "chan"),
            P("chan"),
            P("chan"),
            P(None, "chan"),
            P(("seq", "chan"), "groups"),
        ),
        out_specs=(
            P(("seq", "chan"), "groups"),
            P(("groups", "seq"), None, "chan"),
            P(("groups", "seq"), "chan"),
            P("chan", ("groups", "seq")),
        ),
        check_vma=False,
    )
```

```python
import functools

import jax
import jax.numpy as jnp
from jax import lax
from jax.experimental import pallas as pl
from jax.experimental.pallas import tpu as pltpu
from jax.sharding import PartitionSpec as P

KERNEL_TAPS = 5
DILATION_STEP = 2
CAP = 2
EDGE = 2 * DILATION_STEP
BF = jnp.bfloat16
F32 = jnp.float32
ROOT = 0.7978845608028654
CUBE = 0.044715

VMEM = pl.BlockSpec(memory_space=pltpu.VMEM)
SMEM = pl.BlockSpec(memory_space=pltpu.SMEM)
HBM = pl.BlockSpec(memory_space=pltpu.HBM)


def struct(shape, dtype):
    return jax.ShapeDtypeStruct(shape, dtype)


def launch(body, outs, ins, specs=None, scratch=(), flops=0, moved=0, room=8, name=None):
    return pl.pallas_call(
        body,
        out_shape=outs,
        in_specs=specs or [VMEM] * len(ins),
        out_specs=jax.tree.map(lambda _: VMEM, outs),
        scratch_shapes=list(scratch),
        compiler_params=pltpu.CompilerParams(vmem_limit_bytes=room * 1024 * 1024),
        cost_estimate=pl.CostEstimate(flops=flops, bytes_accessed=moved, transcendentals=0),
        name=name,
    )(*ins)


def dot(a, b, dims=((1,), (0,))):
    return lax.dot_general(a, b, (dims, ((), ())), preferred_element_type=F32)


def wrap(value, count):
    return lax.rem(value + count, count)


def pack_kernel(slabs, rows, block_len, dest_hbm, kept_hbm, x_hbm, cot_ref, *refs):
    outs, (dest_ref, kept_ref, x_ref, parts, sems) = refs[:slabs], refs[slabs:]
    copies = [
        pltpu.make_async_copy(a, b, sems.at[n])
        for n, (a, b) in enumerate(((dest_hbm, dest_ref), (kept_hbm, kept_ref), (x_hbm, x_ref)))
    ]
    for copy in copies:
        copy.start()
    copies[0].wait()
    copies[1].wait()
    me = lax.axis_index("seq")
    payload = CAP * block_len + 16
    feat, count = parts.shape[1:]
    for d in range(slabs):
        parts[d] = cot_ref[:, d * count : (d + 1) * count]
    dest = [jnp.where(dest_ref[r] >= slabs, -100, dest_ref[r]) for r in range(rows)]
    rank, total = [], []
    for r in range(rows):
        before, count = jnp.int32(0), jnp.int32(0)
        for q in range(rows):
            same = (dest[q] == dest[r]).astype(jnp.int32)
            count = count + same
            if q < r:
                before = before + same
        rank.append(before)
        total.append(count)
    columns = rows * block_len
    col = lax.broadcasted_iota(jnp.int32, (1, columns), 1)
    dest_v = jnp.full((1, columns), -100, jnp.int32)
    rank_v = jnp.zeros((1, columns), jnp.int32)
    last_v = jnp.zeros((1, columns), jnp.int32)
    place = jnp.zeros((1, columns), jnp.int32)
    for r in range(rows):
        offset = col - r * block_len
        here = (offset >= 0) & (offset < kept_ref[r]) & (offset < block_len)
        dest_v = jnp.where(here, dest[r], dest_v)
        rank_v = jnp.where(here, rank[r], rank_v)
        last_v = jnp.where(here, (rank[r] == total[r] - 1).astype(jnp.int32), last_v)
        place = jnp.where(here, offset, place)
    row = lax.broadcasted_iota(jnp.int32, (payload, columns), 0)
    line = lax.broadcasted_iota(jnp.int32, (payload, 1), 0)
    base = CAP * block_len
    copies[2].wait()
    x = x_ref[...]
    for k, out in enumerate(outs):
        to = wrap(me + k, slabs)
        key = jnp.where(dest_v == to, rank_v * block_len + place, -1)
        key = jnp.where((dest_v == to + 1) & (rank_v == 0) & (place < EDGE), base + place, key)
        tail = place - (block_len - EDGE)
        key = jnp.where((dest_v == to - 1) & (last_v == 1) & (tail >= 0), base + EDGE + tail, key)
        picker = jnp.where(row == key, 1.0, 0.0).astype(BF)
        rows_out = dot(picker, x)
        for spot, slab in enumerate((to, to - 1, to + 1)):
            number = jnp.int32(0)
            for r in range(rows):
                number = number + (dest[r] == slab).astype(jnp.int32)
            rows_out = jnp.where(line == base + 2 * EDGE + spot, number.astype(F32), rows_out)
        out[:payload] = rows_out.astype(BF)
        piece = parts[to].astype(F32)
        out[payload:] = jnp.concatenate([piece[: feat // 2], piece[feat // 2 :]], axis=1).astype(BF)


def unpack_kernel(slabs, block_len, *refs):
    ins, out, cot = refs[:slabs], refs[slabs], refs[slabs + 1]
    me = lax.axis_index("seq")
    payload = CAP * block_len + 16
    base = CAP * block_len
    length = slabs * block_len
    heads = [r[payload - 16 : payload, :].astype(F32) for r in ins]
    own = [h[2 * EDGE : 2 * EDGE + 1, :payload] for h in heads]
    prev = [h[2 * EDGE + 1 : 2 * EDGE + 2, :payload] for h in heads]
    following = [h[2 * EDGE + 2 : 2 * EDGE + 3, :payload] for h in heads]
    source = [wrap(me - k, slabs) for k in range(slabs)]
    col = lax.broadcasted_iota(jnp.int32, (1, payload), 1)
    slot = jnp.where(col >= block_len, 1, 0)
    place = (col - slot * block_len).astype(F32)
    slot = slot.astype(F32)
    colf = col.astype(F32)
    row = lax.broadcasted_iota(jnp.int32, out.shape[:1] + (payload,), 0).astype(F32)
    total = jnp.zeros(out.shape, F32)
    for k in range(slabs):
        offsets = []
        for counts in (own, prev, following):
            ahead = jnp.zeros((1, payload), F32)
            for q in range(slabs):
                if q != k:
                    ahead = ahead + jnp.where(source[q] < source[k], counts[q], 0.0)
            offsets.append(ahead)
        main = jnp.where(slot < own[k], (offsets[0] + slot) * block_len + place, -1.0)
        right = jnp.where((following[k] > 0.5) & (offsets[2] < 0.5), length + EDGE + colf - base, -1.0)
        left = jnp.where((prev[k] > 0.5) & (offsets[1] + prev[k] > slabs - 0.5), length + colf - base - EDGE, -1.0)
        key = jnp.where(col < base, main, jnp.where(col < base + EDGE, right, jnp.where(col < base + 2 * EDGE, left, -1.0)))
        total = total + dot(jnp.where(row == key, 1.0, 0.0).astype(BF), ins[k][:payload])
        half, count = cot.shape[1] // 2, cot.shape[2]
        piece = ins[k][payload:].astype(F32)
        cot[k, :half] = piece[:, :count].astype(BF)
        cot[k, half:] = piece[:, count:].astype(BF)
    out[...] = total.astype(BF)


def cot_kernel(slabs, chans, *refs):
    ins, (w_ref, gain_ref, out, full) = refs[:chans], refs[chans:]
    me, ch = lax.axis_index("seq"), lax.axis_index("chan")
    feat = ins[0].shape[1]
    for j in range(chans):
        owner = lax.bitwise_xor(ch, j)
        for k in range(slabs):
            begin = pl.multiple_of((wrap(me - k, slabs) * chans + owner) * feat, 16)
            full[pl.ds(begin, feat), :] = ins[j][k]
    out[...] = dot(full[...], w_ref[...], ((0,), (0,))) * gain_ref[...][None, :]


def stage_kernel(w_ref, out, sem):
    copy = pltpu.make_async_copy(w_ref, out, sem)
    copy.start()
    copy.wait()


def quarter_kernel(slabs, chans, *refs):
    xs, pieces = refs[:chans], refs[chans:]
    me, ch = lax.axis_index("seq"), lax.axis_index("chan")
    width = xs[0].shape[1]
    part = pieces[0].shape[0]
    begin = pl.multiple_of(ch * part, 8)
    for k, piece in enumerate(pieces):
        for j in range(chans):

            @pl.when(lax.bitwise_xor(ch, j) == wrap(me + k, slabs))
            def _(piece=piece, j=j):
                piece[...] = xs[j][pl.ds(begin, part), :]


def conv_kernel(chans, *refs):
    xs, (w_ref, bias_ref, pooled_ref, slope_ref), rest = refs[:chans], refs[chans : chans + 4], refs[chans + 4 :]
    full, conv, shifted_sum, lanes = rest
    ch = lax.axis_index("chan")
    rows, width = xs[0].shape
    length = shifted_sum.shape[0]
    for j in range(chans):
        begin = pl.multiple_of(lax.bitwise_xor(ch, j) * width, 128)
        full[:, pl.ds(begin, width)] = xs[j][...]
    x = full[...]
    for t in range(KERNEL_TAPS):
        product = dot(x, w_ref[t])
        conv[0:EDGE] = product[length : length + EDGE]
        conv[EDGE : EDGE + length] = product[:length]
        conv[EDGE + length : 2 * EDGE + length] = product[length + EDGE : length + 2 * EDGE]
        moved = conv[t * DILATION_STEP : t * DILATION_STEP + length]
        if t == 0:
            shifted_sum[...] = moved + bias_ref[...][None, :]
        else:
            shifted_sum[...] += moved
    v = shifted_sum[...]
    th = jnp.tanh(ROOT * (v + CUBE * (v * v * v)))
    half = 0.5 * (1.0 + th)
    slope_ref[...] = half + (0.5 * ROOT) * v * (1.0 - th * th) * (1.0 + (3.0 * CUBE) * (v * v))
    act = v * half
    count = length // 2
    columns = []
    for c in range(width // 128):
        lanes[c] = act[:, c * 128 : (c + 1) * 128]
        columns.append((lanes[c, pl.ds(0, count, stride=2), :] + lanes[c, pl.ds(1, count, stride=2), :]) * 0.5)
    pooled = jnp.concatenate(columns, axis=1)
    pooled_ref[...] = pooled


def sums_kernel(pooled_ref, dxhat_ref, stats_ref):
    pooled = pooled_ref[...]
    count = pooled.shape[0]
    dxhat = dxhat_ref[...]
    sums = [
        jnp.sum(pooled, axis=1, keepdims=True),
        jnp.sum(pooled * pooled, axis=1, keepdims=True),
        jnp.sum(dxhat, axis=1, keepdims=True),
        jnp.sum(dxhat * pooled, axis=1, keepdims=True),
    ]
    lane = lax.broadcasted_iota(jnp.int32, (count, 128), 1)
    table = jnp.zeros((count, 128), F32)
    for n, s in enumerate(sums):
        table = jnp.where(lane == n, s, table)
    padded = stats_ref.shape[1]
    if padded > count:
        table = jnp.concatenate([table, jnp.zeros((padded - count, 128), F32)], axis=0)
    stats_ref[...] = table.T[:8]


def grad_kernel(chans, *refs):
    stats, (pooled_ref, slope_ref, dxhat_ref, gain_ref, low_ref, high_ref, twice) = refs[:chans], refs[chans:]
    count, width = pooled_ref.shape
    total = stats[0][...]
    for s in stats[1:]:
        total = total + s[...]
    total = total * (1.0 / (width * chans))
    table = jnp.concatenate([total, jnp.zeros((120, total.shape[1]), F32)], axis=0).T[:count]
    mean = table[:, 0:1]
    rstd = lax.rsqrt(table[:, 1:2] - mean * mean + 1e-05)
    leading = table[:, 2:3]
    trailing = rstd * (table[:, 3:4] - mean * leading)
    xhat = (pooled_ref[...] - mean) * rstd
    low_ref[:count] = (xhat * gain_ref[...][None, :]).astype(BF)
    half = (0.5 * rstd) * (dxhat_ref[...] - leading - xhat * trailing)
    columns = []
    for c in range(width // 128):
        twice[c, pl.ds(0, count, stride=2), :] = half[:, c * 128 : (c + 1) * 128]
        twice[c, pl.ds(1, count, stride=2), :] = half[:, c * 128 : (c + 1) * 128]
        columns.append(twice[c])
    dy = (jnp.concatenate(columns, axis=1) * slope_ref[...]).astype(BF)
    extra = low_ref.shape[0] - count
    low_ref[count:] = dy[:extra]
    high_ref[...] = dy[extra:]


def dx_kernel(picks, *refs):
    n = len(picks)
    (low_ref, high_ref, left_ref, right_ref, w_ref), outs, (wide, moved) = refs[:5], refs[5 : 5 + n], refs[5 + n :]
    ch = lax.axis_index("chan")
    width = low_ref.shape[1]
    length = moved.shape[1]
    upper = high_ref.shape[0]
    begin = low_ref.shape[0] - (length - upper)
    me = lax.axis_index("seq")
    left = left_ref[upper - 16 : upper].astype(F32)[16 - EDGE :]
    right = right_ref[begin : begin + 16].astype(F32)[:EDGE]
    wide[0:EDGE] = jnp.where(me == 0, 0.0, left)
    wide[EDGE : EDGE + length - upper] = low_ref[begin:].astype(F32)
    wide[EDGE + length - upper : EDGE + length] = high_ref[...].astype(F32)
    wide[EDGE + length : 2 * EDGE + length] = jnp.where(me == lax.axis_size("seq") - 1, 0.0, right)
    for t in range(KERNEL_TAPS):
        begin = 2 * EDGE - t * DILATION_STEP
        moved[t] = wide[begin : begin + length].astype(BF)
    for slot, j in enumerate(picks):
        block = pl.ds(pl.multiple_of(lax.bitwise_xor(ch, j) * width, 16), width)
        total = dot(w_ref[0, block, :], moved[0], ((1,), (1,)))
        for t in range(1, KERNEL_TAPS):
            total = total + dot(w_ref[t, block, :], moved[t], ((1,), (1,)))
        outs[slot][...] = total.astype(outs[slot].dtype)


def transpose_kernel(slabs, chans, x_ref, out, full):
    me = lax.axis_index("seq")
    part = x_ref.shape[2]
    for j in range(chans):
        for k in range(slabs):
            begin = pl.multiple_of((wrap(me - k, slabs) * chans + j) * part, 8)
            full[pl.ds(begin, part), :] = x_ref[j, k]
    out[...] = full[...].T


def dw_kernel(slabs, *refs):
    xt_ref, dys, (out, full, moved) = refs[0], refs[1:-3], refs[-3:]
    me = lax.axis_index("seq")
    width = dys[0].shape[1]
    every = xt_ref.shape[1]
    length = every // slabs
    full[0:8] = jnp.zeros((8, width), F32)
    full[8 + every : 16 + every] = jnp.zeros((8, width), F32)
    half = len(dys) // 2
    upper = dys[half].shape[0]
    extra = length - upper
    lows = [r[dys[0].shape[0] - extra :] for r in dys[:half]]
    highs = [r[...] for r in dys[half:]]
    for k in range(slabs):
        begin = pl.multiple_of(wrap(me - k, slabs) * length + 8, 8)
        full[pl.ds(begin, extra), :] = lows[k].astype(F32)
        full[pl.ds(begin + extra, upper), :] = highs[k].astype(F32)
    xt = xt_ref[...]
    for t in range(KERNEL_TAPS):
        begin = 8 + EDGE - t * DILATION_STEP
        moved[...] = full[begin : begin + every].astype(BF)
        out[t] = dot(xt, moved[...])


def proj_kernel(slabs, chans, *refs):
    cots, normed, rest = refs[:chans], refs[chans : -(chans + 5)], refs[-(chans + 5) :]
    (w_ref, dw_ref), outs, (wide, full, part) = rest[:2], rest[2 : 2 + chans], rest[2 + chans :]
    me, ch = lax.axis_index("seq"), lax.axis_index("chan")
    feat = cots[0].shape[0]
    count = full.shape[0] // slabs
    for j in range(chans):
        wide[pl.ds(pl.multiple_of(lax.bitwise_xor(ch, j) * feat, 8), feat), :] = cots[j][...]
    for k, rows in enumerate([r[:count] for r in normed]):
        full[pl.ds(pl.multiple_of(wrap(me - k, slabs) * count, 8), count), :] = rows
    every = full[...]
    dw_ref[...] = dot(wide[...], every)
    rows = feat * chans
    part[...] = dot(w_ref[pl.ds(pl.multiple_of(me * rows, 8), rows), :], every, ((1,), (1,)))
    for j in range(chans):
        outs[j][...] = part[pl.ds(pl.multiple_of(lax.bitwise_xor(ch, j) * feat, 8), feat), :].astype(outs[j].dtype)


def after(values, *earlier):
    return lax.optimization_barrier((values, earlier))[0]


def swaps(value, count):
    return [value] + [lax.ppermute(value, "chan", [(i, i ^ j) for i in range(count)]) for j in range(1, count)]


def turn(value, k, count):
    return lax.ppermute(value, "seq", [(i, (i + k) % count) for i in range(count)]) if k else value


def relay(value, count):
    near = [(i, i ^ 1) for i in range(count)]
    far = lax.ppermute(value, "chan", [(i, i ^ 2) for i in range(count)])
    return [value, lax.ppermute(value, "chan", near), far, lax.ppermute(far, "chan", near)]


def gather_seq(value, count):
    return [turn(value, k, count) for k in range(count)]


def trade_seq(values, count):
    return [turn(v, k, count) for k, v in enumerate(values)]


def padded(cells, sides, width):
    for axis, dim in sides:
        count = lax.axis_size(axis)
        ends = count - 1
        head = lax.slice_in_dim(cells, 0, width, axis=dim)
        tail = lax.slice_in_dim(cells, cells.shape[dim] - width, cells.shape[dim], axis=dim)
        cells = jnp.concatenate(
            [
                lax.ppermute(tail, axis, [(i, (i + 1) % count) for i in range(ends)]),
                cells,
                lax.ppermute(head, axis, [((i + 1) % count, i) for i in range(ends)]),
            ],
            axis=dim,
        )
    return cells


def smooth_gate(values):
    return jax.nn.gelu(values, approximate=True)


def plain_path(
    x_rows, dest_slab, kept_len, convolution_weight, b_conv, entry_norm_gain, w_proj, g_cot
):
    seq_count = lax.axis_size("seq")
    chan_count = lax.axis_size("chan")
    src_rows, block_len, shard_ch = x_rows.shape
    every_channel = shard_ch * chan_count
    window_width = 2 * DILATION_STEP
    positions = lax.broadcasted_iota(jnp.int32, (src_rows, block_len), 1)
    keep_mask = (positions < kept_len[:, None]).astype(x_rows.dtype)
    masked = (x_rows * keep_mask[:, :, None]).reshape(src_rows, block_len * shard_ch)
    slab_ids = jnp.arange(seq_count + 1, dtype=jnp.int32)
    onehot = (dest_slab[:, None] == slab_ids[None, :]).astype(jnp.int32)
    row_ids = jnp.arange(src_rows, dtype=jnp.int32)
    same = (dest_slab[:, None] == dest_slab[None, :]) & (row_ids[None, :] < row_ids[:, None])
    slot_row = jnp.sum(same.astype(jnp.int32), axis=1)
    target = dest_slab * CAP + slot_row
    send_ids = jnp.arange(seq_count * CAP, dtype=jnp.int32)
    picker = (send_ids[:, None] == target[None, :]).astype(jnp.bfloat16)
    outgoing = jnp.dot(picker, masked, preferred_element_type=jnp.float32).astype(jnp.bfloat16)
    outgoing = outgoing.reshape(seq_count, CAP, block_len * shard_ch)
    sent_counts = jnp.sum(onehot[:, :seq_count], axis=0).astype(jnp.bfloat16).reshape(seq_count, 1)
    arrived, arrived_counts = (
        lax.all_to_all(outgoing, "seq", split_axis=0, concat_axis=0, tiled=True),
        lax.all_to_all(sent_counts, "seq", split_axis=0, concat_axis=0, tiled=True),
    )
    got_counts = arrived_counts[:, 0].astype(jnp.int32)
    src_ids = jnp.arange(seq_count, dtype=jnp.int32)
    offsets = jnp.sum(jnp.where(src_ids[None, :] < src_ids[:, None], got_counts[None, :], 0), axis=1)
    slot_ladder = jnp.arange(CAP, dtype=jnp.int32)
    placed = offsets[:, None] + slot_ladder[None, :]
    placed = jnp.where(slot_ladder[None, :] < got_counts[:, None], placed, -1).reshape(-1)
    block_ids = jnp.arange(seq_count, dtype=jnp.int32)
    arranger = (block_ids[:, None] == placed[None, :]).astype(jnp.bfloat16)
    routed = jnp.dot(
        arranger,
        arrived.reshape(seq_count * CAP, block_len * shard_ch),
        preferred_element_type=jnp.float32,
    )
    routed = routed.astype(jnp.bfloat16).reshape(seq_count * block_len, shard_ch)
    window_length = routed.shape[0]
    pooled_len = window_length // 2
    padded_input = padded(routed, (("seq", 0),), window_width)
    complete_rows = lax.all_gather(padded_input, "chan", axis=1, tiled=True)
    convolved = jnp.zeros((window_length, shard_ch), jnp.float32)
    for kernel_tap_index in range(KERNEL_TAPS):
        convolved = convolved + jnp.dot(
            complete_rows[
                kernel_tap_index * DILATION_STEP : kernel_tap_index * DILATION_STEP + window_length
            ],
            convolution_weight[:, kernel_tap_index, :],
            preferred_element_type=jnp.float32,
        )
    shifted = convolved + b_conv[None, :]
    act, gate_pull = jax.vjp(smooth_gate, shifted)
    paired = act.reshape(pooled_len, 2, shard_ch)
    pooled_output = (paired[:, 0, :] + paired[:, 1, :]) * 0.5
    feat_total = w_proj.shape[0]
    group_feat = feat_total // (seq_count * chan_count)
    block_feat = group_feat * chan_count
    cot_parts = lax.all_to_all(
        g_cot.reshape(group_feat, seq_count, pooled_len), "seq", split_axis=1, concat_axis=0, tiled=True
    ).reshape(seq_count, group_feat, pooled_len)
    cot_slab = lax.all_gather(cot_parts, "chan", axis=1, tiled=True).reshape(feat_total, pooled_len)
    cot_wide = lax.all_gather(g_cot, "chan", axis=0, tiled=True)
    dnormed = jnp.einsum("fp,fd->pd", cot_slab, w_proj, preferred_element_type=jnp.float32)
    dxhat = dnormed * entry_norm_gain[None, :]
    sums = lax.psum(
        jnp.stack(
            [
                jnp.sum(pooled_output, axis=1),
                jnp.sum(pooled_output * pooled_output, axis=1),
                jnp.sum(dxhat, axis=1),
                jnp.sum(dxhat * pooled_output, axis=1),
            ]
        ),
        "chan",
    ) / every_channel
    mean_value = sums[0]
    inverse_deviation = lax.rsqrt(sums[1] - mean_value * mean_value + 1e-05)
    leading = sums[2]
    trailing = inverse_deviation * (sums[3] - mean_value * leading)
    centered_input = (pooled_output - mean_value[:, None]) * inverse_deviation[:, None]
    normalized = (centered_input * entry_norm_gain[None, :]).astype(jnp.bfloat16)
    pooled_gradient = inverse_deviation[:, None] * (
        dxhat - leading[:, None] - centered_input * trailing[:, None]
    )
    dact = jnp.repeat(pooled_gradient * 0.5, 2, axis=0)
    output_gradient = gate_pull(dact)[0].astype(jnp.bfloat16)
    norm_all = lax.all_gather(normalized, "seq", axis=0, tiled=True)
    dy_all = lax.all_gather(output_gradient, "seq", axis=0, tiled=True)
    own_ch = every_channel // seq_count
    x_own = lax.all_to_all(
        complete_rows.reshape(-1, seq_count, own_ch), "seq", split_axis=1, concat_axis=0, tiled=True
    ).reshape(seq_count, -1, own_ch)
    dw_proj = jnp.dot(cot_wide, norm_all, preferred_element_type=jnp.float32)
    w_block = lax.dynamic_slice_in_dim(w_proj, lax.axis_index("seq") * block_feat, block_feat, axis=0)
    qk_part = jnp.einsum("fd,pd->fp", w_block, norm_all, preferred_element_type=jnp.float32)
    qk_out = lax.psum_scatter(qk_part, "chan", scatter_dimension=0, tiled=True).astype(jnp.bfloat16)
    dy_pad = padded(output_gradient, (("seq", 0),), window_width)
    total = jnp.zeros((shard_ch * lax.axis_size("chan"), window_length), jnp.float32)
    for kernel_tap_index in range(KERNEL_TAPS):
        shift_amount = (KERNEL_TAPS - 1 - kernel_tap_index) * DILATION_STEP
        total = total + jnp.einsum(
            "io,po->ip",
            convolution_weight[:, kernel_tap_index, :],
            dy_pad[shift_amount : shift_amount + window_length],
            preferred_element_type=jnp.float32,
        )
    pieces = lax.all_to_all(
        total.astype(jnp.bfloat16).reshape(chan_count, shard_ch, window_length), "chan", split_axis=0, concat_axis=0, tiled=True
    )
    dx_field = jnp.sum(pieces.astype(jnp.float32), axis=0).astype(jnp.bfloat16)
    taps_out = []
    for kernel_tap_index in range(KERNEL_TAPS):
        begin = kernel_tap_index * DILATION_STEP
        taps_out.append(
            jnp.einsum(
                "pi,po->io",
                x_own[:, begin : begin + window_length].reshape(-1, own_ch),
                dy_all,
                preferred_element_type=jnp.float32,
            )
        )
    dw_conv = jnp.stack(taps_out, axis=1)
    return (qk_out, dw_conv, dw_proj, dx_field)


def per_device(x_rows, dest_slab, kept_len, convolution_weight, b_conv, entry_norm_gain, w_proj, g_cot):
    slabs = lax.axis_size("seq")
    chans = lax.axis_size("chan")
    if slabs != 4 or chans != 4:
        return plain_path(x_rows, dest_slab, kept_len, convolution_weight, b_conv, entry_norm_gain, w_proj, g_cot)
    rows, block_len, width = x_rows.shape
    channels = width * chans
    length = slabs * block_len
    count = length // 2
    payload = CAP * block_len + 16
    feat, positions = g_cot.shape
    padded_rows = length + 16
    taps = jnp.transpose(convolution_weight, (1, 0, 2))
    gain = entry_norm_gain
    me = lax.axis_index("seq")
    own = channels // slabs
    part = length // chans
    extra = length // 4

    packed = launch(
        functools.partial(pack_kernel, slabs, rows, block_len),
        [struct((payload + feat // 2, width), BF)] * slabs,
        [dest_slab, kept_len, x_rows.reshape(rows * block_len, width), g_cot],
        specs=[HBM, HBM, HBM, VMEM],
        scratch=[
            pltpu.SMEM((rows,), jnp.int32),
            pltpu.SMEM((rows,), jnp.int32),
            pltpu.VMEM((rows * block_len, width), BF),
            pltpu.VMEM((slabs, feat, count), BF),
            pltpu.SemaphoreType.DMA((3,)),
        ],
        flops=2 * payload * slabs * rows * block_len * width,
        moved=2 * payload * slabs * width,
        name="pack",
    )
    arrived = trade_seq(packed, slabs)

    def staged(*earlier):
        return launch(
            stage_kernel,
            struct(taps.shape, BF),
            [after(taps, *earlier) if earlier else taps],
            specs=[HBM],
            scratch=[pltpu.SemaphoreType.DMA(())],
            moved=4 * channels * width * KERNEL_TAPS,
            name="stage",
        )

    taps_early = staged()
    arrived, taps_early = lax.optimization_barrier((arrived, taps_early))

    routed, cot_mine = launch(
        functools.partial(unpack_kernel, slabs, block_len),
        [struct((padded_rows, width), BF), struct((slabs, feat, count), BF)],
        arrived,
        flops=2 * payload * slabs * padded_rows * width,
        moved=2 * payload * slabs * width,
        name="unpack",
    )
    x_all = relay(routed, chans)
    dxhat = launch(
        functools.partial(cot_kernel, slabs, chans),
        struct((count, width), F32),
        [*swaps(cot_mine, chans), w_proj, gain],
        scratch=[pltpu.VMEM((feat * chans * slabs, count), BF)],
        name="cotangent",
    )
    cot_wide = swaps(g_cot, chans)
    pieces = launch(
        functools.partial(quarter_kernel, slabs, chans), [struct((part, own), BF)] * slabs, x_all, name="quarter"
    )
    traded = trade_seq(pieces, slabs)
    pooled, slope = launch(
        functools.partial(conv_kernel, chans),
        [struct((count, width), F32), struct((length, width), F32)],
        [*x_all, taps_early, b_conv],
        flops=2 * padded_rows * channels * width * KERNEL_TAPS,
        moved=2 * channels * width * KERNEL_TAPS,
        room=16,
        scratch=[
            pltpu.VMEM((padded_rows, channels), BF),
            pltpu.VMEM((length + 2 * EDGE, width), F32),
            pltpu.VMEM((length, width), F32),
            pltpu.VMEM((width // 128, length, 128), F32),
        ],
        name="conv",
    )

    stats = launch(
        sums_kernel, struct((8, -(-count // 128) * 128), F32), [pooled, dxhat], name="sums"
    )
    low, high = launch(
        functools.partial(grad_kernel, chans),
        [struct((count + extra, width), BF), struct((length - extra, width), BF)],
        [*swaps(stats, chans), pooled, slope, dxhat, gain],
        scratch=[pltpu.VMEM((width // 128, length, 128), F32)],
        flops=20 * length * width,
        moved=12 * length * width,
        name="gradient",
    )
    x_own = lax.all_gather(jnp.stack(after(traded, low)), "chan", axis=0, tiled=False)
    x_turned = launch(
        functools.partial(transpose_kernel, slabs, chans),
        struct((own, length * slabs), BF),
        [x_own],
        scratch=[pltpu.VMEM((length * slabs, own), BF)],
        name="turn_x",
    )
    low_all = gather_seq(low, slabs)
    high_all = gather_seq(high, slabs)

    taps_late = staged(low)
    low_far = after(low, low_all[1], low_all[3], high_all[1], high_all[3], taps_late, cot_wide)
    low_near = after(low_far, low_all[2])

    def dx_part(low, picks, dtypes, name):
        return launch(
            functools.partial(dx_kernel, picks),
            [struct((width, length), d) for d in dtypes],
            [low, high, high_all[1], low_all[3], taps_late],
            scratch=[pltpu.VMEM((length + 2 * EDGE, width), F32), pltpu.VMEM((KERNEL_TAPS, length, width), BF)],
            flops=2 * len(picks) * length * width * width * KERNEL_TAPS,
            moved=2 * len(picks) * width * width * KERNEL_TAPS,
            room=14,
            name=name,
        )

    near = [(i, i ^ 1) for i in range(chans)]
    over = [(i, i ^ 2) for i in range(chans)]
    through, across = dx_part(low_far, (3, 2), (BF, F32), "dx_far")
    across = (across + lax.ppermute(through, "chan", near).astype(F32)).astype(BF)
    across = lax.ppermute(across, "chan", over)
    beside, mine_dx = dx_part(low_near, (1, 0), (BF, F32), "dx_near")
    beside = lax.ppermute(beside, "chan", near)
    dx_field = (mine_dx + beside.astype(F32) + across.astype(F32)).astype(BF)

    w_late, x_turned = lax.optimization_barrier((w_proj, x_turned))
    proj = launch(
        functools.partial(proj_kernel, slabs, chans),
        [struct((feat * chans, width), F32), struct((feat, positions), F32)] + [struct((feat, positions), BF)] * (chans - 1),
        [*cot_wide, *low_all, w_late],
        scratch=[
            pltpu.VMEM((feat * chans, positions), BF),
            pltpu.VMEM((positions, width), BF),
            pltpu.VMEM((feat * chans, positions), F32),
        ],
        room=12,
        flops=4 * feat * chans * positions * width,
        moved=4 * feat * chans * width,
        name="projection",
    )
    dw_proj, qk_parts = proj[0], proj[1:]
    qk_got = [lax.ppermute(qk_parts[j], "chan", [(i, i ^ j) for i in range(chans)]) for j in range(1, chans)]
    dw_taps = launch(
        functools.partial(dw_kernel, slabs),
        struct((KERNEL_TAPS, own, width), F32),
        [x_turned, *low_all, *high_all],
        room=16,
        scratch=[pltpu.VMEM((length * slabs + 16, width), F32), pltpu.VMEM((length * slabs, width), BF)],
        flops=2 * length * slabs * own * width * KERNEL_TAPS,
        moved=4 * own * width * KERNEL_TAPS,
        name="dw",
    )
    qk_got, dw_taps = lax.optimization_barrier((qk_got, dw_taps))
    qk_sum = qk_parts[0]
    for got in qk_got:
        qk_sum = qk_sum + got.astype(F32)
    qk_out = qk_sum.astype(BF)
    return (qk_out, jnp.transpose(dw_taps, (1, 0, 2)), dw_proj, dx_field)


def solution(mesh):
    return jax.shard_map(
        per_device,
        mesh=mesh,
        in_specs=(
            P(("groups", "seq"), None, "chan"),
            P(("groups", "seq")),
            P(("groups", "seq")),
            P(None, None, "chan"),
            P("chan"),
            P("chan"),
            P(None, "chan"),
            P(("seq", "chan"), "groups"),
        ),
        out_specs=(
            P(("seq", "chan"), "groups"),
            P(("groups", "seq"), None, "chan"),
            P(("groups", "seq"), "chan"),
            P("chan", ("groups", "seq")),
        ),
        check_vma=False,
    )
```

```python
import functools

import jax
import jax.numpy as jnp
from jax import lax
from jax.experimental import pallas as pl
from jax.experimental.pallas import tpu as pltpu
from jax.sharding import PartitionSpec as P

KERNEL_TAPS = 5
DILATION_STEP = 2
CAP = 2
EDGE = 2 * DILATION_STEP
BF = jnp.bfloat16
F32 = jnp.float32
ROOT = 0.7978845608028654
CUBE = 0.044715

VMEM = pl.BlockSpec(memory_space=pltpu.VMEM)
SMEM = pl.BlockSpec(memory_space=pltpu.SMEM)
HBM = pl.BlockSpec(memory_space=pltpu.HBM)


def struct(shape, dtype):
    return jax.ShapeDtypeStruct(shape, dtype)


def launch(body, outs, ins, specs=None, scratch=(), flops=0, moved=0, room=8, name=None):
    return pl.pallas_call(
        body,
        out_shape=outs,
        in_specs=specs or [VMEM] * len(ins),
        out_specs=jax.tree.map(lambda _: VMEM, outs),
        scratch_shapes=list(scratch),
        compiler_params=pltpu.CompilerParams(vmem_limit_bytes=room * 1024 * 1024),
        cost_estimate=pl.CostEstimate(flops=flops, bytes_accessed=moved, transcendentals=0),
        name=name,
    )(*ins)


def dot(a, b, dims=((1,), (0,))):
    return lax.dot_general(a, b, (dims, ((), ())), preferred_element_type=F32)


def wrap(value, count):
    return lax.rem(value + count, count)


def pack_kernel(slabs, rows, block_len, dest_hbm, kept_hbm, x_hbm, cot_hbm, *refs):
    outs, (dest_ref, kept_ref, x_ref, cot_ref, parts, sems) = refs[:slabs], refs[slabs:]
    copies = [
        pltpu.make_async_copy(a, b, sems.at[n])
        for n, (a, b) in enumerate(((dest_hbm, dest_ref), (kept_hbm, kept_ref), (x_hbm, x_ref), (cot_hbm, cot_ref)))
    ]
    for copy in copies:
        copy.start()
    copies[0].wait()
    copies[1].wait()
    me = lax.axis_index("seq")
    payload = CAP * block_len + 16
    feat, span = parts.shape[1:]
    dest = [jnp.where(dest_ref[r] >= slabs, -100, dest_ref[r]) for r in range(rows)]
    rank, total = [], []
    for r in range(rows):
        before, count = jnp.int32(0), jnp.int32(0)
        for q in range(rows):
            same = (dest[q] == dest[r]).astype(jnp.int32)
            count = count + same
            if q < r:
                before = before + same
        rank.append(before)
        total.append(count)
    columns = rows * block_len
    col = lax.broadcasted_iota(jnp.int32, (1, columns), 1)
    dest_v = jnp.full((1, columns), -100, jnp.int32)
    rank_v = jnp.zeros((1, columns), jnp.int32)
    last_v = jnp.zeros((1, columns), jnp.int32)
    place = jnp.zeros((1, columns), jnp.int32)
    for r in range(rows):
        offset = col - r * block_len
        here = (offset >= 0) & (offset < kept_ref[r]) & (offset < block_len)
        dest_v = jnp.where(here, dest[r], dest_v)
        rank_v = jnp.where(here, rank[r], rank_v)
        last_v = jnp.where(here, (rank[r] == total[r] - 1).astype(jnp.int32), last_v)
        place = jnp.where(here, offset, place)
    row = lax.broadcasted_iota(jnp.int32, (payload, columns), 0)
    line = lax.broadcasted_iota(jnp.int32, (payload, 1), 0)
    base = CAP * block_len
    copies[2].wait()
    copies[3].wait()
    for d in range(slabs):
        parts[d] = cot_ref[:, d * span : (d + 1) * span]
    x = x_ref[...]
    for k, out in enumerate(outs):
        to = wrap(me + k, slabs)
        key = jnp.where(dest_v == to, rank_v * block_len + place, -1)
        key = jnp.where((dest_v == to + 1) & (rank_v == 0) & (place < EDGE), base + place, key)
        tail = place - (block_len - EDGE)
        key = jnp.where((dest_v == to - 1) & (last_v == 1) & (tail >= 0), base + EDGE + tail, key)
        picker = jnp.where(row == key, 1.0, 0.0).astype(BF)
        rows_out = dot(picker, x)
        for spot, slab in enumerate((to, to - 1, to + 1)):
            number = jnp.int32(0)
            for r in range(rows):
                number = number + (dest[r] == slab).astype(jnp.int32)
            rows_out = jnp.where(line == base + 2 * EDGE + spot, number.astype(F32), rows_out)
        out[:payload] = rows_out.astype(BF)
        piece = parts[to].astype(F32)
        out[payload:] = jnp.concatenate([piece[: feat // 2], piece[feat // 2 :]], axis=1).astype(BF)


def unpack_kernel(slabs, block_len, *refs):
    ins, out = refs[:slabs], refs[slabs]
    me = lax.axis_index("seq")
    payload = CAP * block_len + 16
    base = CAP * block_len
    length = slabs * block_len
    heads = [r[payload - 16 : payload, :].astype(F32) for r in ins]
    own = [h[2 * EDGE : 2 * EDGE + 1, :payload] for h in heads]
    prev = [h[2 * EDGE + 1 : 2 * EDGE + 2, :payload] for h in heads]
    following = [h[2 * EDGE + 2 : 2 * EDGE + 3, :payload] for h in heads]
    source = [wrap(me - k, slabs) for k in range(slabs)]
    col = lax.broadcasted_iota(jnp.int32, (1, payload), 1)
    slot = jnp.where(col >= block_len, 1, 0)
    place = (col - slot * block_len).astype(F32)
    slot = slot.astype(F32)
    colf = col.astype(F32)
    shape = (length + 16, out.shape[1])
    row = lax.broadcasted_iota(jnp.int32, (shape[0], payload), 0).astype(F32)
    total = jnp.zeros(shape, F32)
    cot_rows = (out.shape[0] - shape[0]) // slabs
    for k in range(slabs):
        offsets = []
        for counts in (own, prev, following):
            ahead = jnp.zeros((1, payload), F32)
            for q in range(slabs):
                if q != k:
                    ahead = ahead + jnp.where(source[q] < source[k], counts[q], 0.0)
            offsets.append(ahead)
        main = jnp.where(slot < own[k], (offsets[0] + slot) * block_len + place, -1.0)
        right = jnp.where((following[k] > 0.5) & (offsets[2] < 0.5), length + EDGE + colf - base, -1.0)
        left = jnp.where((prev[k] > 0.5) & (offsets[1] + prev[k] > slabs - 0.5), length + colf - base - EDGE, -1.0)
        key = jnp.where(col < base, main, jnp.where(col < base + EDGE, right, jnp.where(col < base + 2 * EDGE, left, -1.0)))
        total = total + dot(jnp.where(row == key, 1.0, 0.0).astype(BF), ins[k][:payload])
        out[shape[0] + k * cot_rows : shape[0] + (k + 1) * cot_rows] = ins[k][payload:]
    out[: shape[0]] = total.astype(BF)


def cot_kernel(slabs, chans, feat, *refs):
    ins, (w_ref, gain_ref, out, full) = refs[:chans], refs[chans:]
    me, ch = lax.axis_index("seq"), lax.axis_index("chan")
    half, count = feat // 2, full.shape[1]
    first = ins[0].shape[0] - slabs * half
    for j in range(chans):
        owner = lax.bitwise_xor(ch, j)
        for k in range(slabs):
            begin = pl.multiple_of((wrap(me - k, slabs) * chans + owner) * feat, 16)
            piece = ins[j][first + k * half : first + (k + 1) * half].astype(F32)
            full[pl.ds(begin, half), :] = piece[:, :count].astype(BF)
            full[pl.ds(begin + half, half), :] = piece[:, count:].astype(BF)
    out[...] = dot(full[...], w_ref[...], ((0,), (0,))) * gain_ref[...][None, :]


def stage_kernel(w_ref, out, sem):
    copy = pltpu.make_async_copy(w_ref, out, sem)
    copy.start()
    copy.wait()


def quarter_kernel(slabs, chans, *refs):
    xs, pieces = refs[:chans], refs[chans:]
    me, ch = lax.axis_index("seq"), lax.axis_index("chan")
    width = xs[0].shape[1]
    part = pieces[0].shape[0]
    begin = pl.multiple_of(ch * part, 8)
    for k, piece in enumerate(pieces):
        for j in range(chans):

            @pl.when(lax.bitwise_xor(ch, j) == wrap(me + k, slabs))
            def _(piece=piece, j=j):
                piece[...] = xs[j][pl.ds(begin, part), :]


def conv_kernel(chans, *refs):
    xs, (w_ref, bias_ref, pooled_ref, slope_ref), rest = refs[:chans], refs[chans : chans + 4], refs[chans + 4 :]
    full, conv, shifted_sum, lanes = rest
    ch = lax.axis_index("chan")
    width = xs[0].shape[1]
    length = shifted_sum.shape[0]
    rows = length + 16
    for j in range(chans):
        begin = pl.multiple_of(lax.bitwise_xor(ch, j) * width, 128)
        full[:, pl.ds(begin, width)] = xs[j][:rows]
    x = full[...]
    for t in range(KERNEL_TAPS):
        product = dot(x, w_ref[t])
        conv[0:EDGE] = product[length : length + EDGE]
        conv[EDGE : EDGE + length] = product[:length]
        conv[EDGE + length : 2 * EDGE + length] = product[length + EDGE : length + 2 * EDGE]
        moved = conv[t * DILATION_STEP : t * DILATION_STEP + length]
        if t == 0:
            shifted_sum[...] = moved + bias_ref[...][None, :]
        else:
            shifted_sum[...] += moved
    v = shifted_sum[...]
    th = jnp.tanh(ROOT * (v + CUBE * (v * v * v)))
    half = 0.5 * (1.0 + th)
    slope_ref[...] = half + (0.5 * ROOT) * v * (1.0 - th * th) * (1.0 + (3.0 * CUBE) * (v * v))
    act = v * half
    count = length // 2
    columns = []
    for c in range(width // 128):
        lanes[c] = act[:, c * 128 : (c + 1) * 128]
        columns.append((lanes[c, pl.ds(0, count, stride=2), :] + lanes[c, pl.ds(1, count, stride=2), :]) * 0.5)
    pooled = jnp.concatenate(columns, axis=1)
    pooled_ref[...] = pooled


def sums_kernel(pooled_ref, dxhat_ref, stats_ref):
    pooled = pooled_ref[...]
    count = pooled.shape[0]
    dxhat = dxhat_ref[...]
    sums = [
        jnp.sum(pooled, axis=1, keepdims=True),
        jnp.sum(pooled * pooled, axis=1, keepdims=True),
        jnp.sum(dxhat, axis=1, keepdims=True),
        jnp.sum(dxhat * pooled, axis=1, keepdims=True),
    ]
    lane = lax.broadcasted_iota(jnp.int32, (count, 128), 1)
    table = jnp.zeros((count, 128), F32)
    for n, s in enumerate(sums):
        table = jnp.where(lane == n, s, table)
    padded = stats_ref.shape[1]
    if padded > count:
        table = jnp.concatenate([table, jnp.zeros((padded - count, 128), F32)], axis=0)
    stats_ref[...] = table.T[:8]


def grad_kernel(chans, *refs):
    stats, (pooled_ref, slope_ref, dxhat_ref, gain_ref, low_ref, high_ref, head_ref, tail_ref, twice) = refs[:chans], refs[chans:]
    count, width = pooled_ref.shape
    total = stats[0][...]
    for s in stats[1:]:
        total = total + s[...]
    total = total * (1.0 / (width * chans))
    table = jnp.concatenate([total, jnp.zeros((120, total.shape[1]), F32)], axis=0).T[:count]
    mean = table[:, 0:1]
    rstd = lax.rsqrt(table[:, 1:2] - mean * mean + 1e-05)
    leading = table[:, 2:3]
    trailing = rstd * (table[:, 3:4] - mean * leading)
    xhat = (pooled_ref[...] - mean) * rstd
    low_ref[:count] = (xhat * gain_ref[...][None, :]).astype(BF)
    half = (0.5 * rstd) * (dxhat_ref[...] - leading - xhat * trailing)
    columns = []
    for c in range(width // 128):
        twice[c, pl.ds(0, count, stride=2), :] = half[:, c * 128 : (c + 1) * 128]
        twice[c, pl.ds(1, count, stride=2), :] = half[:, c * 128 : (c + 1) * 128]
        columns.append(twice[c])
    dy = (jnp.concatenate(columns, axis=1) * slope_ref[...]).astype(BF)
    extra = low_ref.shape[0] - count
    low_ref[count:] = dy[:extra]
    high_ref[...] = dy[extra:]
    head_ref[...] = dy[:16]
    tail_ref[...] = dy[dy.shape[0] - 16 :]


def dx_kernel(picks, *refs):
    n = len(picks)
    (low_ref, high_ref, left_ref, right_ref, w_ref), outs, (wide, moved) = refs[:5], refs[5 : 5 + n], refs[5 + n :]
    ch = lax.axis_index("chan")
    width = low_ref.shape[1]
    length = moved.shape[1]
    upper = high_ref.shape[0]
    begin = low_ref.shape[0] - (length - upper)
    me = lax.axis_index("seq")
    left = left_ref[...].astype(F32)[16 - EDGE :]
    right = right_ref[...].astype(F32)[:EDGE]
    wide[0:EDGE] = jnp.where(me == 0, 0.0, left)
    wide[EDGE : EDGE + length - upper] = low_ref[begin:].astype(F32)
    wide[EDGE + length - upper : EDGE + length] = high_ref[...].astype(F32)
    wide[EDGE + length : 2 * EDGE + length] = jnp.where(me == lax.axis_size("seq") - 1, 0.0, right)
    for t in range(KERNEL_TAPS):
        begin = 2 * EDGE - t * DILATION_STEP
        moved[t] = wide[begin : begin + length].astype(BF)
    for slot, j in enumerate(picks):
        block = pl.ds(pl.multiple_of(lax.bitwise_xor(ch, j) * width, 16), width)
        total = dot(w_ref[0, block, :], moved[0], ((1,), (1,)))
        for t in range(1, KERNEL_TAPS):
            total = total + dot(w_ref[t, block, :], moved[t], ((1,), (1,)))
        outs[slot][...] = total.astype(outs[slot].dtype)


def transpose_kernel(slabs, chans, x_ref, out, full):
    me = lax.axis_index("seq")
    part = x_ref.shape[2]
    for j in range(chans):
        for k in range(slabs):
            begin = pl.multiple_of((wrap(me - k, slabs) * chans + j) * part, 8)
            full[pl.ds(begin, part), :] = x_ref[j, k]
    out[...] = full[...].T


def dw_kernel(slabs, *refs):
    xt_ref, dys, (out, full, moved) = refs[0], refs[1:-3], refs[-3:]
    me = lax.axis_index("seq")
    width = dys[0].shape[1]
    every = xt_ref.shape[1]
    length = every // slabs
    full[0:8] = jnp.zeros((8, width), F32)
    full[8 + every : 16 + every] = jnp.zeros((8, width), F32)
    half = len(dys) // 2
    upper = dys[half].shape[0]
    extra = length - upper
    lows = [r[dys[0].shape[0] - extra :] for r in dys[:half]]
    highs = [r[...] for r in dys[half:]]
    for k in range(slabs):
        begin = pl.multiple_of(lax.bitwise_xor(me, k) * length + 8, 8)
        full[pl.ds(begin, extra), :] = lows[k].astype(F32)
        full[pl.ds(begin + extra, upper), :] = highs[k].astype(F32)
    xt = xt_ref[...]
    for t in range(KERNEL_TAPS):
        begin = 8 + EDGE - t * DILATION_STEP
        moved[...] = full[begin : begin + every].astype(BF)
        out[t] = dot(xt, moved[...])


def proj_kernel(slabs, chans, *refs):
    cots, normed, rest = refs[:chans], refs[chans : -(chans + 5)], refs[-(chans + 5) :]
    (w_ref, dw_ref), outs, (wide, full, part) = rest[:2], rest[2 : 2 + chans], rest[2 + chans :]
    me, ch = lax.axis_index("seq"), lax.axis_index("chan")
    feat = cots[0].shape[0]
    count = full.shape[0] // slabs
    for j in range(chans):
        wide[pl.ds(pl.multiple_of(lax.bitwise_xor(ch, j) * feat, 8), feat), :] = cots[j][...]
    for k, rows in enumerate([r[:count] for r in normed]):
        full[pl.ds(pl.multiple_of(lax.bitwise_xor(me, k) * count, 8), count), :] = rows
    every = full[...]
    dw_ref[...] = dot(wide[...], every)
    rows = feat * chans
    part[...] = dot(w_ref[pl.ds(pl.multiple_of(me * rows, 8), rows), :], every, ((1,), (1,)))
    for j in range(chans):
        outs[j][...] = part[pl.ds(pl.multiple_of(lax.bitwise_xor(ch, j) * feat, 8), feat), :].astype(outs[j].dtype)


def after(values, *earlier):
    return lax.optimization_barrier((values, earlier))[0]


def swaps(value, count):
    return [value] + [lax.ppermute(value, "chan", [(i, i ^ j) for i in range(count)]) for j in range(1, count)]


def turn(value, k, count):
    return lax.ppermute(value, "seq", [(i, (i + k) % count) for i in range(count)]) if k else value


def relay(value, count, axis):
    near = [(i, i ^ 1) for i in range(count)]
    far = lax.ppermute(value, axis, [(i, i ^ 2) for i in range(count)])
    return [value, lax.ppermute(value, axis, near), far, lax.ppermute(far, axis, near)]


def trade_seq(values, count):
    return [turn(v, k, count) for k, v in enumerate(values)]


def padded(cells, sides, width):
    for axis, dim in sides:
        count = lax.axis_size(axis)
        ends = count - 1
        head = lax.slice_in_dim(cells, 0, width, axis=dim)
        tail = lax.slice_in_dim(cells, cells.shape[dim] - width, cells.shape[dim], axis=dim)
        cells = jnp.concatenate(
            [
                lax.ppermute(tail, axis, [(i, (i + 1) % count) for i in range(ends)]),
                cells,
                lax.ppermute(head, axis, [((i + 1) % count, i) for i in range(ends)]),
            ],
            axis=dim,
        )
    return cells


def smooth_gate(values):
    return jax.nn.gelu(values, approximate=True)


def plain_path(
    x_rows, dest_slab, kept_len, convolution_weight, b_conv, entry_norm_gain, w_proj, g_cot
):
    seq_count = lax.axis_size("seq")
    chan_count = lax.axis_size("chan")
    src_rows, block_len, shard_ch = x_rows.shape
    every_channel = shard_ch * chan_count
    window_width = 2 * DILATION_STEP
    positions = lax.broadcasted_iota(jnp.int32, (src_rows, block_len), 1)
    keep_mask = (positions < kept_len[:, None]).astype(x_rows.dtype)
    masked = (x_rows * keep_mask[:, :, None]).reshape(src_rows, block_len * shard_ch)
    slab_ids = jnp.arange(seq_count + 1, dtype=jnp.int32)
    onehot = (dest_slab[:, None] == slab_ids[None, :]).astype(jnp.int32)
    row_ids = jnp.arange(src_rows, dtype=jnp.int32)
    same = (dest_slab[:, None] == dest_slab[None, :]) & (row_ids[None, :] < row_ids[:, None])
    slot_row = jnp.sum(same.astype(jnp.int32), axis=1)
    target = dest_slab * CAP + slot_row
    send_ids = jnp.arange(seq_count * CAP, dtype=jnp.int32)
    picker = (send_ids[:, None] == target[None, :]).astype(jnp.bfloat16)
    outgoing = jnp.dot(picker, masked, preferred_element_type=jnp.float32).astype(jnp.bfloat16)
    outgoing = outgoing.reshape(seq_count, CAP, block_len * shard_ch)
    sent_counts = jnp.sum(onehot[:, :seq_count], axis=0).astype(jnp.bfloat16).reshape(seq_count, 1)
    arrived, arrived_counts = (
        lax.all_to_all(outgoing, "seq", split_axis=0, concat_axis=0, tiled=True),
        lax.all_to_all(sent_counts, "seq", split_axis=0, concat_axis=0, tiled=True),
    )
    got_counts = arrived_counts[:, 0].astype(jnp.int32)
    src_ids = jnp.arange(seq_count, dtype=jnp.int32)
    offsets = jnp.sum(jnp.where(src_ids[None, :] < src_ids[:, None], got_counts[None, :], 0), axis=1)
    slot_ladder = jnp.arange(CAP, dtype=jnp.int32)
    placed = offsets[:, None] + slot_ladder[None, :]
    placed = jnp.where(slot_ladder[None, :] < got_counts[:, None], placed, -1).reshape(-1)
    block_ids = jnp.arange(seq_count, dtype=jnp.int32)
    arranger = (block_ids[:, None] == placed[None, :]).astype(jnp.bfloat16)
    routed = jnp.dot(
        arranger,
        arrived.reshape(seq_count * CAP, block_len * shard_ch),
        preferred_element_type=jnp.float32,
    )
    routed = routed.astype(jnp.bfloat16).reshape(seq_count * block_len, shard_ch)
    window_length = routed.shape[0]
    pooled_len = window_length // 2
    padded_input = padded(routed, (("seq", 0),), window_width)
    complete_rows = lax.all_gather(padded_input, "chan", axis=1, tiled=True)
    convolved = jnp.zeros((window_length, shard_ch), jnp.float32)
    for kernel_tap_index in range(KERNEL_TAPS):
        convolved = convolved + jnp.dot(
            complete_rows[
                kernel_tap_index * DILATION_STEP : kernel_tap_index * DILATION_STEP + window_length
            ],
            convolution_weight[:, kernel_tap_index, :],
            preferred_element_type=jnp.float32,
        )
    shifted = convolved + b_conv[None, :]
    act, gate_pull = jax.vjp(smooth_gate, shifted)
    paired = act.reshape(pooled_len, 2, shard_ch)
    pooled_output = (paired[:, 0, :] + paired[:, 1, :]) * 0.5
    feat_total = w_proj.shape[0]
    group_feat = feat_total // (seq_count * chan_count)
    block_feat = group_feat * chan_count
    cot_parts = lax.all_to_all(
        g_cot.reshape(group_feat, seq_count, pooled_len), "seq", split_axis=1, concat_axis=0, tiled=True
    ).reshape(seq_count, group_feat, pooled_len)
    cot_slab = lax.all_gather(cot_parts, "chan", axis=1, tiled=True).reshape(feat_total, pooled_len)
    cot_wide = lax.all_gather(g_cot, "chan", axis=0, tiled=True)
    dnormed = jnp.einsum("fp,fd->pd", cot_slab, w_proj, preferred_element_type=jnp.float32)
    dxhat = dnormed * entry_norm_gain[None, :]
    sums = lax.psum(
        jnp.stack(
            [
                jnp.sum(pooled_output, axis=1),
                jnp.sum(pooled_output * pooled_output, axis=1),
                jnp.sum(dxhat, axis=1),
                jnp.sum(dxhat * pooled_output, axis=1),
            ]
        ),
        "chan",
    ) / every_channel
    mean_value = sums[0]
    inverse_deviation = lax.rsqrt(sums[1] - mean_value * mean_value + 1e-05)
    leading = sums[2]
    trailing = inverse_deviation * (sums[3] - mean_value * leading)
    centered_input = (pooled_output - mean_value[:, None]) * inverse_deviation[:, None]
    normalized = (centered_input * entry_norm_gain[None, :]).astype(jnp.bfloat16)
    pooled_gradient = inverse_deviation[:, None] * (
        dxhat - leading[:, None] - centered_input * trailing[:, None]
    )
    dact = jnp.repeat(pooled_gradient * 0.5, 2, axis=0)
    output_gradient = gate_pull(dact)[0].astype(jnp.bfloat16)
    norm_all = lax.all_gather(normalized, "seq", axis=0, tiled=True)
    dy_all = lax.all_gather(output_gradient, "seq", axis=0, tiled=True)
    own_ch = every_channel // seq_count
    x_own = lax.all_to_all(
        complete_rows.reshape(-1, seq_count, own_ch), "seq", split_axis=1, concat_axis=0, tiled=True
    ).reshape(seq_count, -1, own_ch)
    dw_proj = jnp.dot(cot_wide, norm_all, preferred_element_type=jnp.float32)
    w_block = lax.dynamic_slice_in_dim(w_proj, lax.axis_index("seq") * block_feat, block_feat, axis=0)
    qk_part = jnp.einsum("fd,pd->fp", w_block, norm_all, preferred_element_type=jnp.float32)
    qk_out = lax.psum_scatter(qk_part, "chan", scatter_dimension=0, tiled=True).astype(jnp.bfloat16)
    dy_pad = padded(output_gradient, (("seq", 0),), window_width)
    total = jnp.zeros((shard_ch * lax.axis_size("chan"), window_length), jnp.float32)
    for kernel_tap_index in range(KERNEL_TAPS):
        shift_amount = (KERNEL_TAPS - 1 - kernel_tap_index) * DILATION_STEP
        total = total + jnp.einsum(
            "io,po->ip",
            convolution_weight[:, kernel_tap_index, :],
            dy_pad[shift_amount : shift_amount + window_length],
            preferred_element_type=jnp.float32,
        )
    pieces = lax.all_to_all(
        total.astype(jnp.bfloat16).reshape(chan_count, shard_ch, window_length), "chan", split_axis=0, concat_axis=0, tiled=True
    )
    dx_field = jnp.sum(pieces.astype(jnp.float32), axis=0).astype(jnp.bfloat16)
    taps_out = []
    for kernel_tap_index in range(KERNEL_TAPS):
        begin = kernel_tap_index * DILATION_STEP
        taps_out.append(
            jnp.einsum(
                "pi,po->io",
                x_own[:, begin : begin + window_length].reshape(-1, own_ch),
                dy_all,
                preferred_element_type=jnp.float32,
            )
        )
    dw_conv = jnp.stack(taps_out, axis=1)
    return (qk_out, dw_conv, dw_proj, dx_field)


def per_device(x_rows, dest_slab, kept_len, convolution_weight, b_conv, entry_norm_gain, w_proj, g_cot):
    slabs = lax.axis_size("seq")
    chans = lax.axis_size("chan")
    if slabs != 4 or chans != 4:
        return plain_path(x_rows, dest_slab, kept_len, convolution_weight, b_conv, entry_norm_gain, w_proj, g_cot)
    rows, block_len, width = x_rows.shape
    channels = width * chans
    length = slabs * block_len
    count = length // 2
    payload = CAP * block_len + 16
    feat, positions = g_cot.shape
    padded_rows = length + 16
    taps = jnp.transpose(convolution_weight, (1, 0, 2))
    gain = entry_norm_gain
    me = lax.axis_index("seq")
    own = channels // slabs
    part = length // chans
    extra = length // 4

    packed = launch(
        functools.partial(pack_kernel, slabs, rows, block_len),
        [struct((payload + feat // 2, width), BF)] * slabs,
        [dest_slab, kept_len, x_rows.reshape(rows * block_len, width), g_cot],
        specs=[HBM] * 4,
        scratch=[
            pltpu.SMEM((rows,), jnp.int32),
            pltpu.SMEM((rows,), jnp.int32),
            pltpu.VMEM((rows * block_len, width), BF),
            pltpu.VMEM((feat, positions), BF),
            pltpu.VMEM((slabs, feat, count), BF),
            pltpu.SemaphoreType.DMA((4,)),
        ],
        flops=2 * payload * slabs * rows * block_len * width,
        moved=2 * payload * slabs * width,
        room=60,
        name="pack",
    )
    arrived = trade_seq(packed, slabs)

    def staged(*earlier):
        return launch(
            stage_kernel,
            struct(taps.shape, BF),
            [after(taps, *earlier) if earlier else taps],
            specs=[HBM],
            scratch=[pltpu.SemaphoreType.DMA(())],
            moved=4 * channels * width * KERNEL_TAPS,
            name="stage",
        )

    taps_early = staged()
    cot_wide = swaps(after(g_cot, packed[0]), chans)
    arrived, taps_early, cot_wide = lax.optimization_barrier((arrived, taps_early, cot_wide))

    routed = launch(
        functools.partial(unpack_kernel, slabs, block_len),
        struct((padded_rows + slabs * feat // 2, width), BF),
        arrived,
        flops=2 * payload * slabs * padded_rows * width,
        moved=2 * payload * slabs * width,
        name="unpack",
    )
    x_all = relay(routed, chans, "chan")
    dxhat = launch(
        functools.partial(cot_kernel, slabs, chans, feat),
        struct((count, width), F32),
        [*x_all, w_proj, gain],
        scratch=[pltpu.VMEM((feat * chans * slabs, count), BF)],
        name="cotangent",
    )
    pieces = launch(
        functools.partial(quarter_kernel, slabs, chans), [struct((part, own), BF)] * slabs, x_all, name="quarter"
    )
    traded = trade_seq(pieces, slabs)
    pooled, slope = launch(
        functools.partial(conv_kernel, chans),
        [struct((count, width), F32), struct((length, width), F32)],
        [*x_all, taps_early, b_conv],
        flops=2 * padded_rows * channels * width * KERNEL_TAPS,
        moved=2 * channels * width * KERNEL_TAPS,
        room=16,
        scratch=[
            pltpu.VMEM((padded_rows, channels), BF),
            pltpu.VMEM((length + 2 * EDGE, width), F32),
            pltpu.VMEM((length, width), F32),
            pltpu.VMEM((width // 128, length, 128), F32),
        ],
        name="conv",
    )

    stats = launch(
        sums_kernel, struct((8, -(-count // 128) * 128), F32), [pooled, dxhat], name="sums"
    )
    low, high, head, tail = launch(
        functools.partial(grad_kernel, chans),
        [struct((n, width), BF) for n in (count + extra, length - extra, 16, 16)],
        [*swaps(stats, chans), pooled, slope, dxhat, gain],
        scratch=[pltpu.VMEM((width // 128, length, 128), F32)],
        flops=20 * length * width,
        moved=12 * length * width,
        name="gradient",
    )
    x_own = lax.all_gather(jnp.stack(after(traded, low)), "chan", axis=0, tiled=False)
    x_turned = launch(
        functools.partial(transpose_kernel, slabs, chans),
        struct((own, length * slabs), BF),
        [x_own],
        scratch=[pltpu.VMEM((length * slabs, own), BF)],
        name="turn_x",
    )
    low_all = relay(low, slabs, "seq")
    high_all = relay(high, slabs, "seq")
    from_left, from_right = turn(tail, 1, slabs), turn(head, slabs - 1, slabs)

    taps_late = staged(low)
    low_far = after(low, low_all[1], low_all[2], taps_late)
    low_near = after(low_far, low_all[3], high_all[2])

    def dx_part(low, picks, dtypes, name):
        return launch(
            functools.partial(dx_kernel, picks),
            [struct((width, length), d) for d in dtypes],
            [low, high, from_left, from_right, taps_late],
            scratch=[pltpu.VMEM((length + 2 * EDGE, width), F32), pltpu.VMEM((KERNEL_TAPS, length, width), BF)],
            flops=2 * len(picks) * length * width * width * KERNEL_TAPS,
            moved=2 * len(picks) * width * width * KERNEL_TAPS,
            room=14,
            name=name,
        )

    near = [(i, i ^ 1) for i in range(chans)]
    over = [(i, i ^ 2) for i in range(chans)]
    through, across = dx_part(low_far, (3, 2), (BF, F32), "dx_far")
    across = (across + lax.ppermute(through, "chan", near).astype(F32)).astype(BF)
    across = lax.ppermute(across, "chan", over)
    beside, mine_dx = dx_part(low_near, (1, 0), (BF, F32), "dx_near")
    beside = lax.ppermute(beside, "chan", near)

    w_late, x_turned = lax.optimization_barrier((w_proj, x_turned))
    proj = launch(
        functools.partial(proj_kernel, slabs, chans),
        [struct((feat * chans, width), F32), struct((feat, positions), F32)] + [struct((feat, positions), BF)] * (chans - 1),
        [*cot_wide, *low_all, w_late],
        scratch=[
            pltpu.VMEM((feat * chans, positions), BF),
            pltpu.VMEM((positions, width), BF),
            pltpu.VMEM((feat * chans, positions), F32),
        ],
        room=12,
        flops=4 * feat * chans * positions * width,
        moved=4 * feat * chans * width,
        name="projection",
    )
    dw_proj, qk_parts = proj[0], proj[1:]
    qk_got = [lax.ppermute(qk_parts[j], "chan", [(i, i ^ j) for i in range(chans)]) for j in range(1, chans)]
    dw_taps = launch(
        functools.partial(dw_kernel, slabs),
        struct((KERNEL_TAPS, own, width), F32),
        [x_turned, *low_all, *high_all],
        room=16,
        scratch=[pltpu.VMEM((length * slabs + 16, width), F32), pltpu.VMEM((length * slabs, width), BF)],
        flops=2 * length * slabs * own * width * KERNEL_TAPS,
        moved=4 * own * width * KERNEL_TAPS,
        name="dw",
    )
    qk_got, beside, across, dw_taps = lax.optimization_barrier((qk_got, beside, across, dw_taps))
    dx_field = (mine_dx + beside.astype(F32) + across.astype(F32)).astype(BF)
    qk_sum = qk_parts[0]
    for got in qk_got:
        qk_sum = qk_sum + got.astype(F32)
    qk_out = qk_sum.astype(BF)
    return (qk_out, jnp.transpose(dw_taps, (1, 0, 2)), dw_proj, dx_field)


def solution(mesh):
    return jax.shard_map(
        per_device,
        mesh=mesh,
        in_specs=(
            P(("groups", "seq"), None, "chan"),
            P(("groups", "seq")),
            P(("groups", "seq")),
            P(None, None, "chan"),
            P("chan"),
            P("chan"),
            P(None, "chan"),
            P(("seq", "chan"), "groups"),
        ),
        out_specs=(
            P(("seq", "chan"), "groups"),
            P(("groups", "seq"), None, "chan"),
            P(("groups", "seq"), "chan"),
            P("chan", ("groups", "seq")),
        ),
        check_vma=False,
    )
```

```python
import functools

import jax
import jax.numpy as jnp
from jax import lax
from jax.experimental import pallas as pl
from jax.experimental.pallas import tpu as pltpu
from jax.sharding import PartitionSpec as P

KERNEL_TAPS = 5
DILATION_STEP = 2
CAP = 2
EDGE = 2 * DILATION_STEP
BF = jnp.bfloat16
F32 = jnp.float32
ROOT = 0.7978845608028654
CUBE = 0.044715

VMEM = pl.BlockSpec(memory_space=pltpu.VMEM)
SMEM = pl.BlockSpec(memory_space=pltpu.SMEM)
HBM = pl.BlockSpec(memory_space=pltpu.HBM)


def struct(shape, dtype):
    return jax.ShapeDtypeStruct(shape, dtype)


def launch(body, outs, ins, specs=None, scratch=(), flops=0, moved=0, room=8, name=None):
    return pl.pallas_call(
        body,
        out_shape=outs,
        in_specs=specs or [VMEM] * len(ins),
        out_specs=jax.tree.map(lambda _: VMEM, outs),
        scratch_shapes=list(scratch),
        compiler_params=pltpu.CompilerParams(vmem_limit_bytes=room * 1024 * 1024),
        cost_estimate=pl.CostEstimate(flops=flops, bytes_accessed=moved, transcendentals=0),
        name=name,
    )(*ins)


def dot(a, b, dims=((1,), (0,))):
    return lax.dot_general(a, b, (dims, ((), ())), preferred_element_type=F32)


def wrap(value, count):
    return lax.rem(value + count, count)


def pack_kernel(slabs, rows, block_len, dest_hbm, kept_hbm, x_hbm, cot_hbm, *refs):
    outs, (dest_ref, kept_ref, x_ref, cot_ref, parts, sems) = refs[:slabs], refs[slabs:]
    copies = [
        pltpu.make_async_copy(a, b, sems.at[n])
        for n, (a, b) in enumerate(((dest_hbm, dest_ref), (kept_hbm, kept_ref), (x_hbm, x_ref), (cot_hbm, cot_ref)))
    ]
    for copy in copies:
        copy.start()
    copies[0].wait()
    copies[1].wait()
    me = lax.axis_index("seq")
    payload = CAP * block_len + 16
    feat, span = parts.shape[1:]
    dest = [jnp.where(dest_ref[r] >= slabs, -100, dest_ref[r]) for r in range(rows)]
    rank, total = [], []
    for r in range(rows):
        before, count = jnp.int32(0), jnp.int32(0)
        for q in range(rows):
            same = (dest[q] == dest[r]).astype(jnp.int32)
            count = count + same
            if q < r:
                before = before + same
        rank.append(before)
        total.append(count)
    columns = rows * block_len
    col = lax.broadcasted_iota(jnp.int32, (1, columns), 1)
    dest_v = jnp.full((1, columns), -100, jnp.int32)
    rank_v = jnp.zeros((1, columns), jnp.int32)
    last_v = jnp.zeros((1, columns), jnp.int32)
    place = jnp.zeros((1, columns), jnp.int32)
    for r in range(rows):
        offset = col - r * block_len
        here = (offset >= 0) & (offset < kept_ref[r]) & (offset < block_len)
        dest_v = jnp.where(here, dest[r], dest_v)
        rank_v = jnp.where(here, rank[r], rank_v)
        last_v = jnp.where(here, (rank[r] == total[r] - 1).astype(jnp.int32), last_v)
        place = jnp.where(here, offset, place)
    row = lax.broadcasted_iota(jnp.int32, (payload, columns), 0)
    line = lax.broadcasted_iota(jnp.int32, (payload, 1), 0)
    base = CAP * block_len
    copies[2].wait()
    copies[3].wait()
    for d in range(slabs):
        parts[d] = cot_ref[:, d * span : (d + 1) * span]
    x = x_ref[...]
    for k, out in enumerate(outs):
        to = wrap(me + k, slabs)
        key = jnp.where(dest_v == to, rank_v * block_len + place, -1)
        key = jnp.where((dest_v == to + 1) & (rank_v == 0) & (place < EDGE), base + place, key)
        tail = place - (block_len - EDGE)
        key = jnp.where((dest_v == to - 1) & (last_v == 1) & (tail >= 0), base + EDGE + tail, key)
        picker = jnp.where(row == key, 1.0, 0.0).astype(BF)
        rows_out = dot(picker, x)
        for spot, slab in enumerate((to, to - 1, to + 1)):
            number = jnp.int32(0)
            for r in range(rows):
                number = number + (dest[r] == slab).astype(jnp.int32)
            rows_out = jnp.where(line == base + 2 * EDGE + spot, number.astype(F32), rows_out)
        out[:payload] = rows_out.astype(BF)
        piece = parts[to].astype(F32)
        out[payload:] = jnp.concatenate([piece[: feat // 2], piece[feat // 2 :]], axis=1).astype(BF)


def unpack_kernel(slabs, block_len, *refs):
    ins, out = refs[:slabs], refs[slabs]
    me = lax.axis_index("seq")
    payload = CAP * block_len + 16
    base = CAP * block_len
    length = slabs * block_len
    heads = [r[payload - 16 : payload, :].astype(F32) for r in ins]
    own = [h[2 * EDGE : 2 * EDGE + 1, :payload] for h in heads]
    prev = [h[2 * EDGE + 1 : 2 * EDGE + 2, :payload] for h in heads]
    following = [h[2 * EDGE + 2 : 2 * EDGE + 3, :payload] for h in heads]
    source = [wrap(me - k, slabs) for k in range(slabs)]
    col = lax.broadcasted_iota(jnp.int32, (1, payload), 1)
    slot = jnp.where(col >= block_len, 1, 0)
    place = (col - slot * block_len).astype(F32)
    slot = slot.astype(F32)
    colf = col.astype(F32)
    shape = (length + 16, out.shape[1])
    row = lax.broadcasted_iota(jnp.int32, (shape[0], payload), 0).astype(F32)
    total = jnp.zeros(shape, F32)
    cot_rows = (out.shape[0] - shape[0]) // slabs
    for k in range(slabs):
        offsets = []
        for counts in (own, prev, following):
            ahead = jnp.zeros((1, payload), F32)
            for q in range(slabs):
                if q != k:
                    ahead = ahead + jnp.where(source[q] < source[k], counts[q], 0.0)
            offsets.append(ahead)
        main = jnp.where(slot < own[k], (offsets[0] + slot) * block_len + place, -1.0)
        right = jnp.where((following[k] > 0.5) & (offsets[2] < 0.5), length + EDGE + colf - base, -1.0)
        left = jnp.where((prev[k] > 0.5) & (offsets[1] + prev[k] > slabs - 0.5), length + colf - base - EDGE, -1.0)
        key = jnp.where(col < base, main, jnp.where(col < base + EDGE, right, jnp.where(col < base + 2 * EDGE, left, -1.0)))
        total = total + dot(jnp.where(row == key, 1.0, 0.0).astype(BF), ins[k][:payload])
        out[shape[0] + k * cot_rows : shape[0] + (k + 1) * cot_rows] = ins[k][payload:]
    out[: shape[0]] = total.astype(BF)


def cot_kernel(slabs, chans, feat, *refs):
    ins, (w_ref, gain_ref, out, full) = refs[:chans], refs[chans:]
    me, ch = lax.axis_index("seq"), lax.axis_index("chan")
    half, count = feat // 2, full.shape[1]
    first = ins[0].shape[0] - slabs * half
    for j in range(chans):
        owner = lax.bitwise_xor(ch, j)
        for k in range(slabs):
            begin = pl.multiple_of((wrap(me - k, slabs) * chans + owner) * feat, 16)
            piece = ins[j][first + k * half : first + (k + 1) * half].astype(F32)
            full[pl.ds(begin, half), :] = piece[:, :count].astype(BF)
            full[pl.ds(begin + half, half), :] = piece[:, count:].astype(BF)
    out[...] = dot(full[...], w_ref[...], ((0,), (0,))) * gain_ref[...][None, :]


def stage_kernel(w_ref, out, sem):
    copy = pltpu.make_async_copy(w_ref, out, sem)
    copy.start()
    copy.wait()


def quarter_kernel(slabs, chans, *refs):
    xs, pieces = refs[:chans], refs[chans:]
    me, ch = lax.axis_index("seq"), lax.axis_index("chan")
    width = xs[0].shape[1]
    part = pieces[0].shape[0]
    begin = pl.multiple_of(ch * part, 8)
    for k, piece in enumerate(pieces):
        for j in range(chans):

            @pl.when(lax.bitwise_xor(ch, j) == wrap(me + k, slabs))
            def _(piece=piece, j=j):
                piece[...] = xs[j][pl.ds(begin, part), :]


def conv_kernel(chans, *refs):
    xs, (w_ref, bias_ref, pooled_ref, slope_ref), rest = refs[:chans], refs[chans : chans + 4], refs[chans + 4 :]
    full, conv, shifted_sum, lanes = rest
    ch = lax.axis_index("chan")
    width = xs[0].shape[1]
    length = shifted_sum.shape[0]
    rows = length + 16
    for j in range(chans):
        begin = pl.multiple_of(lax.bitwise_xor(ch, j) * width, 128)
        full[:, pl.ds(begin, width)] = xs[j][:rows]
    x = full[...]
    for t in range(KERNEL_TAPS):
        product = dot(x, w_ref[t])
        conv[0:EDGE] = product[length : length + EDGE]
        conv[EDGE : EDGE + length] = product[:length]
        conv[EDGE + length : 2 * EDGE + length] = product[length + EDGE : length + 2 * EDGE]
        moved = conv[t * DILATION_STEP : t * DILATION_STEP + length]
        if t == 0:
            shifted_sum[...] = moved + bias_ref[...][None, :]
        else:
            shifted_sum[...] += moved
    v = shifted_sum[...]
    th = jnp.tanh(ROOT * (v + CUBE * (v * v * v)))
    half = 0.5 * (1.0 + th)
    slope_ref[...] = half + (0.5 * ROOT) * v * (1.0 - th * th) * (1.0 + (3.0 * CUBE) * (v * v))
    act = v * half
    count = length // 2
    columns = []
    for c in range(width // 128):
        lanes[c] = act[:, c * 128 : (c + 1) * 128]
        columns.append((lanes[c, pl.ds(0, count, stride=2), :] + lanes[c, pl.ds(1, count, stride=2), :]) * 0.5)
    pooled = jnp.concatenate(columns, axis=1)
    pooled_ref[...] = pooled


def sums_kernel(pooled_ref, dxhat_ref, stats_ref):
    pooled = pooled_ref[...]
    count = pooled.shape[0]
    dxhat = dxhat_ref[...]
    sums = [
        jnp.sum(pooled, axis=1, keepdims=True),
        jnp.sum(pooled * pooled, axis=1, keepdims=True),
        jnp.sum(dxhat, axis=1, keepdims=True),
        jnp.sum(dxhat * pooled, axis=1, keepdims=True),
    ]
    lane = lax.broadcasted_iota(jnp.int32, (count, 128), 1)
    table = jnp.zeros((count, 128), F32)
    for n, s in enumerate(sums):
        table = jnp.where(lane == n, s, table)
    padded = stats_ref.shape[1]
    if padded > count:
        table = jnp.concatenate([table, jnp.zeros((padded - count, 128), F32)], axis=0)
    stats_ref[...] = table.T[:8]


def grad_kernel(chans, *refs):
    stats, (pooled_ref, slope_ref, dxhat_ref, gain_ref, low_ref, high_ref, head_ref, tail_ref, twice) = refs[:chans], refs[chans:]
    count, width = pooled_ref.shape
    total = stats[0][...]
    for s in stats[1:]:
        total = total + s[...]
    total = total * (1.0 / (width * chans))
    table = jnp.concatenate([total, jnp.zeros((120, total.shape[1]), F32)], axis=0).T[:count]
    mean = table[:, 0:1]
    rstd = lax.rsqrt(table[:, 1:2] - mean * mean + 1e-05)
    leading = table[:, 2:3]
    trailing = rstd * (table[:, 3:4] - mean * leading)
    xhat = (pooled_ref[...] - mean) * rstd
    low_ref[:count] = (xhat * gain_ref[...][None, :]).astype(BF)
    half = (0.5 * rstd) * (dxhat_ref[...] - leading - xhat * trailing)
    columns = []
    for c in range(width // 128):
        twice[c, pl.ds(0, count, stride=2), :] = half[:, c * 128 : (c + 1) * 128]
        twice[c, pl.ds(1, count, stride=2), :] = half[:, c * 128 : (c + 1) * 128]
        columns.append(twice[c])
    dy = (jnp.concatenate(columns, axis=1) * slope_ref[...]).astype(BF)
    extra = low_ref.shape[0] - count
    low_ref[count:] = dy[:extra]
    high_ref[...] = dy[extra:]
    head_ref[...] = dy[:16]
    tail_ref[...] = dy[dy.shape[0] - 16 :]


def dx_kernel(picks, *refs):
    n = len(picks)
    (low_ref, high_ref, left_ref, right_ref, w_ref), outs, (wide, moved) = refs[:5], refs[5 : 5 + n], refs[5 + n :]
    ch = lax.axis_index("chan")
    width = low_ref.shape[1]
    length = moved.shape[1]
    upper = high_ref.shape[0]
    begin = low_ref.shape[0] - (length - upper)
    me = lax.axis_index("seq")
    left = left_ref[...].astype(F32)[16 - EDGE :]
    right = right_ref[...].astype(F32)[:EDGE]
    wide[0:EDGE] = jnp.where(me == 0, 0.0, left)
    wide[EDGE : EDGE + length - upper] = low_ref[begin:].astype(F32)
    wide[EDGE + length - upper : EDGE + length] = high_ref[...].astype(F32)
    wide[EDGE + length : 2 * EDGE + length] = jnp.where(me == lax.axis_size("seq") - 1, 0.0, right)
    for t in range(KERNEL_TAPS):
        begin = 2 * EDGE - t * DILATION_STEP
        moved[t] = wide[begin : begin + length].astype(BF)
    for slot, j in enumerate(picks):
        block = pl.ds(pl.multiple_of(lax.bitwise_xor(ch, j) * width, 16), width)
        total = dot(w_ref[0, block, :], moved[0], ((1,), (1,)))
        for t in range(1, KERNEL_TAPS):
            total = total + dot(w_ref[t, block, :], moved[t], ((1,), (1,)))
        outs[slot][...] = total.astype(outs[slot].dtype)


def transpose_kernel(slabs, chans, x_ref, out, full):
    me = lax.axis_index("seq")
    part = x_ref.shape[2]
    for j in range(chans):
        for k in range(slabs):
            begin = pl.multiple_of((wrap(me - k, slabs) * chans + j) * part, 8)
            full[pl.ds(begin, part), :] = x_ref[j, k]
    out[...] = full[...].T


def dw_kernel(slabs, *refs):
    xt_ref, dys, (out, full, moved) = refs[0], refs[1:-3], refs[-3:]
    me = lax.axis_index("seq")
    width = dys[0].shape[1]
    every = xt_ref.shape[1]
    length = every // slabs
    full[0:8] = jnp.zeros((8, width), F32)
    full[8 + every : 16 + every] = jnp.zeros((8, width), F32)
    half = len(dys) // 2
    upper = dys[half].shape[0]
    extra = length - upper
    lows = [r[dys[0].shape[0] - extra :] for r in dys[:half]]
    highs = [r[...] for r in dys[half:]]
    for k in range(slabs):
        begin = pl.multiple_of(lax.bitwise_xor(me, k) * length + 8, 8)
        full[pl.ds(begin, extra), :] = lows[k].astype(F32)
        full[pl.ds(begin + extra, upper), :] = highs[k].astype(F32)
    xt = xt_ref[...]
    for t in range(KERNEL_TAPS):
        begin = 8 + EDGE - t * DILATION_STEP
        moved[...] = full[begin : begin + every].astype(BF)
        out[t] = dot(xt, moved[...])


def finish_kernel(*refs):
    ins, (dx_ref, qk_ref) = refs[:-2], refs[-2:]
    dx_ref[...] = (ins[0][...] + ins[1][...].astype(F32) + ins[2][...].astype(F32)).astype(BF)
    total = ins[3][...]
    for part in ins[4:]:
        total = total + part[...].astype(F32)
    qk_ref[...] = total.astype(BF)


def proj_kernel(slabs, chans, *refs):
    cots, normed, rest = refs[:chans], refs[chans : -(chans + 5)], refs[-(chans + 5) :]
    (w_ref, dw_ref), outs, (wide, full, part) = rest[:2], rest[2 : 2 + chans], rest[2 + chans :]
    me, ch = lax.axis_index("seq"), lax.axis_index("chan")
    feat = cots[0].shape[0]
    count = full.shape[0] // slabs
    for j in range(chans):
        wide[pl.ds(pl.multiple_of(lax.bitwise_xor(ch, j) * feat, 8), feat), :] = cots[j][...]
    for k, rows in enumerate([r[:count] for r in normed]):
        full[pl.ds(pl.multiple_of(lax.bitwise_xor(me, k) * count, 8), count), :] = rows
    every = full[...]
    dw_ref[...] = dot(wide[...], every)
    rows = feat * chans
    part[...] = dot(w_ref[pl.ds(pl.multiple_of(me * rows, 8), rows), :], every, ((1,), (1,)))
    for j in range(chans):
        outs[j][...] = part[pl.ds(pl.multiple_of(lax.bitwise_xor(ch, j) * feat, 8), feat), :].astype(outs[j].dtype)


def after(values, *earlier):
    return lax.optimization_barrier((values, earlier))[0]


def swaps(value, count):
    return [value] + [lax.ppermute(value, "chan", [(i, i ^ j) for i in range(count)]) for j in range(1, count)]


def turn(value, k, count):
    return lax.ppermute(value, "seq", [(i, (i + k) % count) for i in range(count)]) if k else value


def relay(value, count, axis):
    near = [(i, i ^ 1) for i in range(count)]
    far = lax.ppermute(value, axis, [(i, i ^ 2) for i in range(count)])
    return [value, lax.ppermute(value, axis, near), far, lax.ppermute(far, axis, near)]


def trade_seq(values, count):
    return [turn(v, k, count) for k, v in enumerate(values)]


def padded(cells, sides, width):
    for axis, dim in sides:
        count = lax.axis_size(axis)
        ends = count - 1
        head = lax.slice_in_dim(cells, 0, width, axis=dim)
        tail = lax.slice_in_dim(cells, cells.shape[dim] - width, cells.shape[dim], axis=dim)
        cells = jnp.concatenate(
            [
                lax.ppermute(tail, axis, [(i, (i + 1) % count) for i in range(ends)]),
                cells,
                lax.ppermute(head, axis, [((i + 1) % count, i) for i in range(ends)]),
            ],
            axis=dim,
        )
    return cells


def smooth_gate(values):
    return jax.nn.gelu(values, approximate=True)


def plain_path(
    x_rows, dest_slab, kept_len, convolution_weight, b_conv, entry_norm_gain, w_proj, g_cot
):
    seq_count = lax.axis_size("seq")
    chan_count = lax.axis_size("chan")
    src_rows, block_len, shard_ch = x_rows.shape
    every_channel = shard_ch * chan_count
    window_width = 2 * DILATION_STEP
    positions = lax.broadcasted_iota(jnp.int32, (src_rows, block_len), 1)
    keep_mask = (positions < kept_len[:, None]).astype(x_rows.dtype)
    masked = (x_rows * keep_mask[:, :, None]).reshape(src_rows, block_len * shard_ch)
    slab_ids = jnp.arange(seq_count + 1, dtype=jnp.int32)
    onehot = (dest_slab[:, None] == slab_ids[None, :]).astype(jnp.int32)
    row_ids = jnp.arange(src_rows, dtype=jnp.int32)
    same = (dest_slab[:, None] == dest_slab[None, :]) & (row_ids[None, :] < row_ids[:, None])
    slot_row = jnp.sum(same.astype(jnp.int32), axis=1)
    target = dest_slab * CAP + slot_row
    send_ids = jnp.arange(seq_count * CAP, dtype=jnp.int32)
    picker = (send_ids[:, None] == target[None, :]).astype(jnp.bfloat16)
    outgoing = jnp.dot(picker, masked, preferred_element_type=jnp.float32).astype(jnp.bfloat16)
    outgoing = outgoing.reshape(seq_count, CAP, block_len * shard_ch)
    sent_counts = jnp.sum(onehot[:, :seq_count], axis=0).astype(jnp.bfloat16).reshape(seq_count, 1)
    arrived, arrived_counts = (
        lax.all_to_all(outgoing, "seq", split_axis=0, concat_axis=0, tiled=True),
        lax.all_to_all(sent_counts, "seq", split_axis=0, concat_axis=0, tiled=True),
    )
    got_counts = arrived_counts[:, 0].astype(jnp.int32)
    src_ids = jnp.arange(seq_count, dtype=jnp.int32)
    offsets = jnp.sum(jnp.where(src_ids[None, :] < src_ids[:, None], got_counts[None, :], 0), axis=1)
    slot_ladder = jnp.arange(CAP, dtype=jnp.int32)
    placed = offsets[:, None] + slot_ladder[None, :]
    placed = jnp.where(slot_ladder[None, :] < got_counts[:, None], placed, -1).reshape(-1)
    block_ids = jnp.arange(seq_count, dtype=jnp.int32)
    arranger = (block_ids[:, None] == placed[None, :]).astype(jnp.bfloat16)
    routed = jnp.dot(
        arranger,
        arrived.reshape(seq_count * CAP, block_len * shard_ch),
        preferred_element_type=jnp.float32,
    )
    routed = routed.astype(jnp.bfloat16).reshape(seq_count * block_len, shard_ch)
    window_length = routed.shape[0]
    pooled_len = window_length // 2
    padded_input = padded(routed, (("seq", 0),), window_width)
    complete_rows = lax.all_gather(padded_input, "chan", axis=1, tiled=True)
    convolved = jnp.zeros((window_length, shard_ch), jnp.float32)
    for kernel_tap_index in range(KERNEL_TAPS):
        convolved = convolved + jnp.dot(
            complete_rows[
                kernel_tap_index * DILATION_STEP : kernel_tap_index * DILATION_STEP + window_length
            ],
            convolution_weight[:, kernel_tap_index, :],
            preferred_element_type=jnp.float32,
        )
    shifted = convolved + b_conv[None, :]
    act, gate_pull = jax.vjp(smooth_gate, shifted)
    paired = act.reshape(pooled_len, 2, shard_ch)
    pooled_output = (paired[:, 0, :] + paired[:, 1, :]) * 0.5
    feat_total = w_proj.shape[0]
    group_feat = feat_total // (seq_count * chan_count)
    block_feat = group_feat * chan_count
    cot_parts = lax.all_to_all(
        g_cot.reshape(group_feat, seq_count, pooled_len), "seq", split_axis=1, concat_axis=0, tiled=True
    ).reshape(seq_count, group_feat, pooled_len)
    cot_slab = lax.all_gather(cot_parts, "chan", axis=1, tiled=True).reshape(feat_total, pooled_len)
    cot_wide = lax.all_gather(g_cot, "chan", axis=0, tiled=True)
    dnormed = jnp.einsum("fp,fd->pd", cot_slab, w_proj, preferred_element_type=jnp.float32)
    dxhat = dnormed * entry_norm_gain[None, :]
    sums = lax.psum(
        jnp.stack(
            [
                jnp.sum(pooled_output, axis=1),
                jnp.sum(pooled_output * pooled_output, axis=1),
                jnp.sum(dxhat, axis=1),
                jnp.sum(dxhat * pooled_output, axis=1),
            ]
        ),
        "chan",
    ) / every_channel
    mean_value = sums[0]
    inverse_deviation = lax.rsqrt(sums[1] - mean_value * mean_value + 1e-05)
    leading = sums[2]
    trailing = inverse_deviation * (sums[3] - mean_value * leading)
    centered_input = (pooled_output - mean_value[:, None]) * inverse_deviation[:, None]
    normalized = (centered_input * entry_norm_gain[None, :]).astype(jnp.bfloat16)
    pooled_gradient = inverse_deviation[:, None] * (
        dxhat - leading[:, None] - centered_input * trailing[:, None]
    )
    dact = jnp.repeat(pooled_gradient * 0.5, 2, axis=0)
    output_gradient = gate_pull(dact)[0].astype(jnp.bfloat16)
    norm_all = lax.all_gather(normalized, "seq", axis=0, tiled=True)
    dy_all = lax.all_gather(output_gradient, "seq", axis=0, tiled=True)
    own_ch = every_channel // seq_count
    x_own = lax.all_to_all(
        complete_rows.reshape(-1, seq_count, own_ch), "seq", split_axis=1, concat_axis=0, tiled=True
    ).reshape(seq_count, -1, own_ch)
    dw_proj = jnp.dot(cot_wide, norm_all, preferred_element_type=jnp.float32)
    w_block = lax.dynamic_slice_in_dim(w_proj, lax.axis_index("seq") * block_feat, block_feat, axis=0)
    qk_part = jnp.einsum("fd,pd->fp", w_block, norm_all, preferred_element_type=jnp.float32)
    qk_out = lax.psum_scatter(qk_part, "chan", scatter_dimension=0, tiled=True).astype(jnp.bfloat16)
    dy_pad = padded(output_gradient, (("seq", 0),), window_width)
    total = jnp.zeros((shard_ch * lax.axis_size("chan"), window_length), jnp.float32)
    for kernel_tap_index in range(KERNEL_TAPS):
        shift_amount = (KERNEL_TAPS - 1 - kernel_tap_index) * DILATION_STEP
        total = total + jnp.einsum(
            "io,po->ip",
            convolution_weight[:, kernel_tap_index, :],
            dy_pad[shift_amount : shift_amount + window_length],
            preferred_element_type=jnp.float32,
        )
    pieces = lax.all_to_all(
        total.astype(jnp.bfloat16).reshape(chan_count, shard_ch, window_length), "chan", split_axis=0, concat_axis=0, tiled=True
    )
    dx_field = jnp.sum(pieces.astype(jnp.float32), axis=0).astype(jnp.bfloat16)
    taps_out = []
    for kernel_tap_index in range(KERNEL_TAPS):
        begin = kernel_tap_index * DILATION_STEP
        taps_out.append(
            jnp.einsum(
                "pi,po->io",
                x_own[:, begin : begin + window_length].reshape(-1, own_ch),
                dy_all,
                preferred_element_type=jnp.float32,
            )
        )
    dw_conv = jnp.stack(taps_out, axis=1)
    return (qk_out, dw_conv, dw_proj, dx_field)


def per_device(x_rows, dest_slab, kept_len, convolution_weight, b_conv, entry_norm_gain, w_proj, g_cot):
    slabs = lax.axis_size("seq")
    chans = lax.axis_size("chan")
    if slabs != 4 or chans != 4:
        return plain_path(x_rows, dest_slab, kept_len, convolution_weight, b_conv, entry_norm_gain, w_proj, g_cot)
    rows, block_len, width = x_rows.shape
    channels = width * chans
    length = slabs * block_len
    count = length // 2
    payload = CAP * block_len + 16
    feat, positions = g_cot.shape
    padded_rows = length + 16
    taps = jnp.transpose(convolution_weight, (1, 0, 2))
    gain = entry_norm_gain
    me = lax.axis_index("seq")
    own = channels // slabs
    part = length // chans
    extra = length // 4

    packed = launch(
        functools.partial(pack_kernel, slabs, rows, block_len),
        [struct((payload + feat // 2, width), BF)] * slabs,
        [dest_slab, kept_len, x_rows.reshape(rows * block_len, width), g_cot],
        specs=[HBM] * 4,
        scratch=[
            pltpu.SMEM((rows,), jnp.int32),
            pltpu.SMEM((rows,), jnp.int32),
            pltpu.VMEM((rows * block_len, width), BF),
            pltpu.VMEM((feat, positions), BF),
            pltpu.VMEM((slabs, feat, count), BF),
            pltpu.SemaphoreType.DMA((4,)),
        ],
        flops=2 * payload * slabs * rows * block_len * width,
        moved=2 * payload * slabs * width,
        room=60,
        name="pack",
    )
    arrived = trade_seq(packed, slabs)

    def staged(*earlier):
        return launch(
            stage_kernel,
            struct(taps.shape, BF),
            [after(taps, *earlier) if earlier else taps],
            specs=[HBM],
            scratch=[pltpu.SemaphoreType.DMA(())],
            moved=4 * channels * width * KERNEL_TAPS,
            name="stage",
        )

    taps_early = staged()
    cot_wide = swaps(after(g_cot, packed[0]), chans)
    arrived, taps_early, cot_wide = lax.optimization_barrier((arrived, taps_early, cot_wide))

    routed = launch(
        functools.partial(unpack_kernel, slabs, block_len),
        struct((padded_rows + slabs * feat // 2, width), BF),
        arrived,
        flops=2 * payload * slabs * padded_rows * width,
        moved=2 * payload * slabs * width,
        name="unpack",
    )
    x_all = relay(routed, chans, "chan")
    dxhat = launch(
        functools.partial(cot_kernel, slabs, chans, feat),
        struct((count, width), F32),
        [*x_all, w_proj, gain],
        scratch=[pltpu.VMEM((feat * chans * slabs, count), BF)],
        name="cotangent",
    )
    pieces = launch(
        functools.partial(quarter_kernel, slabs, chans), [struct((part, own), BF)] * slabs, x_all, name="quarter"
    )
    traded = trade_seq(pieces, slabs)
    pooled, slope = launch(
        functools.partial(conv_kernel, chans),
        [struct((count, width), F32), struct((length, width), F32)],
        [*x_all, taps_early, b_conv],
        flops=2 * padded_rows * channels * width * KERNEL_TAPS,
        moved=2 * channels * width * KERNEL_TAPS,
        room=16,
        scratch=[
            pltpu.VMEM((padded_rows, channels), BF),
            pltpu.VMEM((length + 2 * EDGE, width), F32),
            pltpu.VMEM((length, width), F32),
            pltpu.VMEM((width // 128, length, 128), F32),
        ],
        name="conv",
    )

    stats = launch(
        sums_kernel, struct((8, -(-count // 128) * 128), F32), [pooled, dxhat], name="sums"
    )
    low, high, head, tail = launch(
        functools.partial(grad_kernel, chans),
        [struct((n, width), BF) for n in (count + extra, length - extra, 16, 16)],
        [*swaps(stats, chans), pooled, slope, dxhat, gain],
        scratch=[pltpu.VMEM((width // 128, length, 128), F32)],
        flops=20 * length * width,
        moved=12 * length * width,
        name="gradient",
    )
    x_own = lax.all_gather(jnp.stack(after(traded, low)), "chan", axis=0, tiled=False)
    x_turned = launch(
        functools.partial(transpose_kernel, slabs, chans),
        struct((own, length * slabs), BF),
        [x_own],
        scratch=[pltpu.VMEM((length * slabs, own), BF)],
        name="turn_x",
    )
    low_all = relay(low, slabs, "seq")
    high_all = relay(after(high, low_all[2]), slabs, "seq")
    from_left, from_right = turn(tail, 1, slabs), turn(head, slabs - 1, slabs)

    taps_late = staged(low)
    low_far = after(low, low_all[1], low_all[2], taps_late)
    low_near = after(low_far, low_all[3], high_all[2])

    def dx_part(low, picks, dtypes, name):
        return launch(
            functools.partial(dx_kernel, picks),
            [struct((width, length), d) for d in dtypes],
            [low, high, from_left, from_right, taps_late],
            scratch=[pltpu.VMEM((length + 2 * EDGE, width), F32), pltpu.VMEM((KERNEL_TAPS, length, width), BF)],
            flops=2 * len(picks) * length * width * width * KERNEL_TAPS,
            moved=2 * len(picks) * width * width * KERNEL_TAPS,
            room=14,
            name=name,
        )

    near = [(i, i ^ 1) for i in range(chans)]
    over = [(i, i ^ 2) for i in range(chans)]
    through, across = dx_part(low_far, (3, 2), (BF, F32), "dx_far")
    across = (across + lax.ppermute(through, "chan", near).astype(F32)).astype(BF)
    across = lax.ppermute(across, "chan", over)
    beside, mine_dx = dx_part(low_near, (1, 0), (BF, F32), "dx_near")
    beside = lax.ppermute(beside, "chan", near)

    w_late, x_turned = lax.optimization_barrier((w_proj, x_turned))
    proj = launch(
        functools.partial(proj_kernel, slabs, chans),
        [struct((feat * chans, width), F32), struct((feat, positions), F32)] + [struct((feat, positions), BF)] * (chans - 1),
        [*cot_wide, *low_all, w_late],
        scratch=[
            pltpu.VMEM((feat * chans, positions), BF),
            pltpu.VMEM((positions, width), BF),
            pltpu.VMEM((feat * chans, positions), F32),
        ],
        room=12,
        flops=4 * feat * chans * positions * width,
        moved=4 * feat * chans * width,
        name="projection",
    )
    dw_proj, qk_parts = proj[0], proj[1:]
    qk_got = [lax.ppermute(qk_parts[j], "chan", [(i, i ^ j) for i in range(chans)]) for j in range(1, chans)]
    dw_taps = launch(
        functools.partial(dw_kernel, slabs),
        struct((KERNEL_TAPS, own, width), F32),
        [x_turned, *low_all, *high_all],
        room=16,
        scratch=[pltpu.VMEM((length * slabs + 16, width), F32), pltpu.VMEM((length * slabs, width), BF)],
        flops=2 * length * slabs * own * width * KERNEL_TAPS,
        moved=4 * own * width * KERNEL_TAPS,
        name="dw",
    )
    qk_got, beside, across, dw_taps = lax.optimization_barrier((qk_got, beside, across, dw_taps))
    dx_field, qk_out = launch(
        finish_kernel,
        [struct((width, length), BF), struct((feat, positions), BF)],
        [mine_dx, beside, across, qk_parts[0], *qk_got],
        name="finish",
    )
    return (qk_out, jnp.transpose(dw_taps, (1, 0, 2)), dw_proj, dx_field)


def solution(mesh):
    return jax.shard_map(
        per_device,
        mesh=mesh,
        in_specs=(
            P(("groups", "seq"), None, "chan"),
            P(("groups", "seq")),
            P(("groups", "seq")),
            P(None, None, "chan"),
            P("chan"),
            P("chan"),
            P(None, "chan"),
            P(("seq", "chan"), "groups"),
        ),
        out_specs=(
            P(("seq", "chan"), "groups"),
            P(("groups", "seq"), None, "chan"),
            P(("groups", "seq"), "chan"),
            P("chan", ("groups", "seq")),
        ),
        check_vma=False,
    )
```
